256 devices in a mesh: chan: 8 (over z_lo, core), region: 32 (over x, y, z_hi).
Axes of the slice: x: 4, y: 4, z: 8 (z_hi: 2, z_lo: 4; z = z_hi * 4 + z_lo), core: 2. Of those that a mesh axis runs over, the one named last changes fastest.
Arguments:
- latent: bfloat16 [32, 24, 24, 12, 128], P('region'), may hold values from -6 to 6
- cond_scale: float32 [128], replicated, may hold values from 0.5 to 1.5
- cond_shift: float32 [128], replicated, may hold values from -3 to 3
- fine_weight: bfloat16 [3, 3, 3, 128, 128], replicated, may hold values from -0.109375 to 0.109375
- fine_bias: float32 [128], replicated, may hold values from -3 to 3
- proj_weight: bfloat16 [8192, 1024], P(('chan', 'region')), may hold values from -0.0625 to 0.0625
- proj_bias: float32 [1024], replicated, may hold values from -3 to 3
- bottle_weight: bfloat16 [27, 1024, 1024], P(None, 'chan'), may hold values from -0.0390625 to 0.0390625
- bottle_bias: float32 [1024], replicated, may hold values from -3 to 3
- guide: float32 [1], replicated, may hold values from 1.5 to 4
Outputs:
- guided: bfloat16 [32, 6, 6, 3, 1024], P('region', None, None, None, 'chan')
The draws below stay inside these ranges and needn't reach their ends.
All inputs are finite; a program needn't handle non-finite values.
Results may differ from the reference program's by a relative error of at most 0.012.
The reference program's roundings to bfloat16 on the way (of `slab`, `inputs`, `hidden` and `coarse`) count: a program that leaves them out, or rounds other values in their place, can miss the bound.
Values may be sent and summed in bfloat16 or wider, within the bound.
A program may use at most 128 MiB of HBM per device.

```python
import jax
import jax.numpy as jnp
from jax import lax

FINE_WIDTH = 128
COARSE_WIDTH = 1024
TILE_SIDE = 12
STRIDE = 4
REGIONS_Y = 4
REGIONS_Z = 2
N_REGION = 32


def steps_of(key, dims, split, low, top_value):
    level, own = 1.0, jax.random.fold_in(key, 6)
    for position, shards_of in split:
        draws = jnp.exp(jax.random.uniform(jax.random.fold_in(own, position), (shards_of,), jnp.float32, low / len(split), top_value / len(split)))
        level = level * jnp.repeat(draws, dims[position] // shards_of).reshape([-1 if axis == position else 1 for axis in range(len(dims))])
    return level


def noise(key, shape, width, most, pieces=(), held_as=jnp.bfloat16):
    gain = steps_of(key, shape, pieces, -0.22, 0.18) if pieces else 1.0
    result = jax.random.normal(key, shape, jnp.float32) * width * gain
    return jnp.minimum(jnp.maximum(result, -most), most).astype(held_as)


def setup_inputs(seed: int = 0) -> dict:
    key_list = jax.random.split(jax.random.key(seed), 11)
    return {
        "latent": noise(key_list[0], (N_REGION, 2 * TILE_SIDE, 2 * TILE_SIDE, TILE_SIDE, FINE_WIDTH), 1.0, 6.0, ((0, 32),)),
        "cond_scale": jnp.clip(1.0 + 0.1 * jax.random.normal(key_list[1], (FINE_WIDTH,), jnp.float32), 0.5, 1.5),
        "cond_shift": noise(key_list[2], (FINE_WIDTH,), 0.5, 3.0, (), jnp.float32),
        "fine_weight": noise(key_list[3], (3, 3, 3, FINE_WIDTH, FINE_WIDTH), (27 * FINE_WIDTH) ** -0.5, 0.109375),
        "fine_bias": noise(key_list[4], (FINE_WIDTH,), 0.5, 3.0, (), jnp.float32),
        "proj_weight": noise(key_list[5], (FINE_WIDTH * STRIDE ** 3, COARSE_WIDTH), (FINE_WIDTH * STRIDE ** 3) ** -0.5, 0.0625, ((0, 256),)),
        "proj_bias": noise(key_list[6], (COARSE_WIDTH,), 0.5, 3.0, (), jnp.float32),
        "bottle_weight": noise(key_list[7], (27, COARSE_WIDTH, COARSE_WIDTH), (27 * COARSE_WIDTH) ** -0.5, 0.0390625, ((1, 8),)),
        "bottle_bias": noise(key_list[8], (COARSE_WIDTH,), 0.5, 3.0, (), jnp.float32),
        "guide": jnp.clip(jax.random.uniform(key_list[9], (1,), jnp.float32, 1.5, 4.0), 1.5, 4.0),
    }


def blocks_to_slab(array, side_x, side_y, side_z):
    count_x = array.shape[0] // (REGIONS_Y * REGIONS_Z)
    grid = array.reshape(count_x, REGIONS_Y, REGIONS_Z, side_x, side_y, side_z, array.shape[-1])
    grid = grid.transpose(0, 3, 1, 4, 2, 5, 6)
    return grid.reshape(count_x * side_x, REGIONS_Y * side_y, REGIONS_Z * side_z, array.shape[-1])


def slab_to_blocks(field, side_x, side_y, side_z):
    count_x = field.shape[0] // side_x
    grid = field.reshape(count_x, side_x, REGIONS_Y, side_y, REGIONS_Z, side_z, field.shape[-1])
    grid = grid.transpose(0, 2, 4, 1, 3, 5, 6)
    return grid.reshape(count_x * REGIONS_Y * REGIONS_Z, side_x, side_y, side_z, field.shape[-1])


def conv_three(field, kernel):
    return lax.conv_general_dilated(field, kernel, (1, 1, 1), "SAME",
                                    dimension_numbers=("NDHWC", "DHWIO", "NDHWC"),
                                    precision=lax.Precision.HIGHEST)


def reference(latent, cond_scale, cond_shift, fine_weight, fine_bias, proj_weight, proj_bias, bottle_weight, bottle_bias, guide):
    side = TILE_SIDE
    slab = blocks_to_slab(latent, 2 * side, 2 * side, side).astype(jnp.float32)
    shaped = (slab * cond_scale + cond_shift).astype(jnp.bfloat16)
    shaped = lax.optimization_barrier(shaped).astype(jnp.float32)
    inputs = jnp.stack([slab, shaped])
    hidden = jax.nn.silu(conv_three(inputs, fine_weight.astype(jnp.float32)) + fine_bias).astype(jnp.bfloat16)
    width_x, width_y, width_z = hidden.shape[1] // STRIDE, hidden.shape[2] // STRIDE, hidden.shape[3] // STRIDE
    grid = hidden.reshape(2, width_x, STRIDE, width_y, STRIDE, width_z, STRIDE, FINE_WIDTH)
    grid = grid.transpose(0, 1, 3, 5, 7, 2, 4, 6).reshape(2 * width_x * width_y * width_z, FINE_WIDTH * STRIDE ** 3)
    coarse = (jnp.dot(grid, proj_weight, preferred_element_type=jnp.float32) + proj_bias).astype(jnp.bfloat16)
    coarse = coarse.reshape(2, width_x, width_y, width_z, COARSE_WIDTH).astype(jnp.float32)
    kernel = bottle_weight.reshape(3, 3, 3, COARSE_WIDTH, COARSE_WIDTH).astype(jnp.float32)
    bottle = jax.nn.silu(conv_three(coarse, kernel) + bottle_bias)
    guided = (bottle[0] + guide[0] * (bottle[1] - bottle[0])).astype(jnp.bfloat16)
    cells = side // STRIDE
    return slab_to_blocks(guided, 2 * cells, 2 * cells, cells)
```

```python
import functools

import jax
import jax.numpy as jnp
from jax import lax
from jax.experimental import pallas as pl
from jax.experimental.pallas import tpu as pltpu
from jax.sharding import PartitionSpec as P

F32 = jnp.float32
BF16 = jnp.bfloat16
SIDES = (-1, 1)


def place_of():
    c = lax.axis_index("chan")
    r = lax.axis_index("region")
    return c // 2, c % 2, r // 8, r // 2 % 4, r % 2


def device_at(zlo, core, x, y, zhi):
    return (zlo * 2 + core, (x * 4 + y) * 2 + zhi)


class Mail:
    def __init__(self, send, recv):
        self.send, self.recv, self.used = send, recv, 0
        self.all = []

    def post(self, src, dst, target):
        copy = pltpu.make_async_remote_copy(
            src_ref=src,
            dst_ref=dst,
            send_sem=self.send.at[self.used],
            recv_sem=self.recv.at[self.used],
            device_id=target,
            device_id_type=pl.DeviceIdType.MESH,
        )
        self.used += 1
        copy.start()
        self.all.append(copy)
        return copy


def silu(v):
    return v / (1.0 + jnp.exp(-v))


def kernel(
    lat, scale, shift, fw, fbias, pw, pbias, bw, bbias, guide,
    out,
    L, G, A, FW, WZ, H, HID, WR, WP, PM, BW, CF, FR, FB, T, TS, RB, YB,
    HX, HY, HC, ZS, ZSY, ZP, ZX, ZY, ZC,
    CX, CY, CC, CZ, CZX, CZY, CZC,
    lsem, ssem, rsem,
):
    zlo, core, x, y, zhi = place_of()
    mail = Mail(ssem, rsem)

    def near(sx, sy, sz):
        return device_at(zlo, core, (x + sx) % 4, (y + sy) % 4, (zhi + sz) % 2)

    def line(dz):
        z = (zhi * 4 + zlo + dz) % 8
        return device_at(z % 4, core, x, y, z // 4)

    partner = device_at(zlo, 1 - core, x, y, zhi)

    loads = []

    def load(src, dst):
        copy = pltpu.make_async_copy(src, dst, lsem.at[len(loads)])
        copy.start()
        loads.append(copy)
        return copy

    load_lat = load(lat.at[0], L)
    load_fw = load(fw, FW)
    me_ch = lambda: (core, x, y)
    own_w = load(
        pw.at[:, pl.ds(pl.multiple_of(zlo * 256, 256), 256)],
        WR.at[zlo, core, x, y, pl.ds(pl.multiple_of(zhi * 32, 32), 32)],
    )
    own_b = [
        load(
            bw.at[:, :, pl.ds(pl.multiple_of((2 * z + core) * 128, 128), 128)],
            BW.at[:, pl.ds(pl.multiple_of(core * 128, 128), 128), z * 128 : z * 128 + 128],
        )
        for z in range(4)
    ]

    barrier = pltpu.get_barrier_semaphore()
    friends = [near(sx, sy, 0) for sx in (-1, 0, 1) for sy in (-1, 0, 1) if sx or sy]
    friends += [near(sx, sy, 1) for sx in (-1, 0, 1) for sy in (-1, 0, 1)]
    friends += [near(2, 0, 0), near(0, 2, 0)]
    friends += [line(d) for d in (1, 2, 3, 5, 6, 7)]
    friends += [partner]
    for friend in friends:
        pl.semaphore_signal(barrier, inc=1, device_id=friend, device_id_type=pl.DeviceIdType.MESH)
    pl.semaphore_wait(barrier, len(friends))

    edge = {-1: 23, 1: 0}
    slot = {-1: 0, 1: 1}
    fine = []
    for s in SIDES:
        fine.append(mail.post(lat.at[0, edge[s]], HX.at[slot[s]], near(-s, 0, 0)))
        fine.append(mail.post(lat.at[0, :, edge[s]], HY.at[slot[s]], near(0, -s, 0)))
    for sx in SIDES:
        for sy in SIDES:
            fine.append(
                mail.post(
                    lat.at[0, edge[sx], edge[sy]],
                    HC.at[slot[sx] * 2 + slot[sy]],
                    near(-sx, -sy, 0),
                )
            )

    rows_here = pl.ds(pl.multiple_of(zhi * 32, 32), 32)
    first = []
    for d in (4, 3, 5, 2, 6, 1, 7):
        target = line(d)
        z_there = (zhi * 4 + zlo + d) % 8 % 4
        first.append(
            mail.post(
                pw.at[:, pl.ds(pl.multiple_of(z_there * 256, 256), 256)],
                WR.at[zlo, core, x, y, rows_here],
                target,
            )
        )

    load_lat.wait()

    def widen(i, carry):
        for j in range(24):
            G[pl.ds((i + 1) * 416 + (j + 1) * 16 + 1, 12), :] = L[i, j].astype(F32)
        return carry

    lax.fori_loop(0, 24, widen, 0)

    def edge_rows(start, stride):
        low = G[pl.ds(start + 1, 24, stride=stride), :]
        high = G[pl.ds(start + 12, 24, stride=stride), :]
        return jnp.where(zhi == 0, high, low).astype(BF16)

    def plane(i, carry):
        ZS[i] = edge_rows((i + 1) * 416 + 16, 16)
        return carry

    lax.fori_loop(0, 24, plane, 0)
    ZSY[0] = edge_rows(416 + 16, 416)
    ZSY[1] = edge_rows(416 + 24 * 16, 416)

    half = pl.ds(pl.multiple_of(core * 12, 12), 12)
    face = mail.post(ZS.at[half], ZP.at[half], near(0, 0, 1))
    above = []
    strip = {-1: 1, 1: 0}
    for s in SIDES:
        above.append(mail.post(ZS.at[edge[s]], ZX.at[slot[s]], near(-s, 0, 1)))
        above.append(mail.post(ZSY.at[strip[s]], ZY.at[slot[s]], near(0, -s, 1)))
    for sx in SIDES:
        for sy in SIDES:
            above.append(
                mail.post(
                    ZSY.at[strip[sy]], ZC.at[slot[sx] * 2 + slot[sy]], near(-sx, -sy, 1)
                )
            )

    swap_b = [
        mail.post(
            bw.at[:, :, pl.ds(pl.multiple_of((2 * z + 1 - core) * 128, 128), 128)],
            BW.at[:, pl.ds(pl.multiple_of(core * 128, 128), 128), z * 128 : z * 128 + 128],
            partner,
        )
        for z in range(4)
    ]

    load_fw.wait()
    for dx in range(3):
        for dz in range(3):
            for step in range(4):
                for o in range(2):
                    dy = step - o
                    here = (dx * 3 + dz, slice(step * 128, step * 128 + 128), slice(o * 128, o * 128 + 128))
                    if 0 <= dy < 3:
                        WZ[here] = FW[dx, dy, dz]
                    else:
                        WZ[here] = jnp.zeros((128, 128), BF16)
    row = lax.broadcasted_iota(jnp.int32, (256, 256), 0)
    col = lax.broadcasted_iota(jnp.int32, (256, 256), 1)
    PM[...] = jnp.where(col == (row & 15) * 16 + (row >> 4), 1.0, 0.0).astype(BF16)
    H[:, 384:416, :] = jnp.zeros((4, 32, 128), F32)

    own_w.wait()
    for copy in first:
        copy.wait_recv()
    second = []
    for d in (2, 1, 3):
        second.append(
            mail.post(WR.at[0:2, core, x, y], WR.at[0:2, core, x, y], near(d, 0, 0))
        )
        second.append(
            mail.post(WR.at[2:4, core, x, y], WR.at[2:4, core, x, y], near(0, d, 0))
        )

    for copy in fine:
        copy.wait_recv()

    def border(j, carry):
        for s in (0, 1):
            at = s * 25
            G[pl.ds(at * 416 + (j + 1) * 16 + 1, 12), :] = HX[s, j].astype(F32)
            G[pl.ds((j + 1) * 416 + at * 16 + 1, 12), :] = HY[s, j].astype(F32)
        return carry

    lax.fori_loop(0, 24, border, 0)
    for sx in (0, 1):
        for sy in (0, 1):
            G[sx * 25 * 416 + sy * 25 * 16 + 1 : sx * 25 * 416 + sy * 25 * 16 + 13, :] = HC[
                sx * 2 + sy
            ].astype(F32)

    face.wait_recv()
    relay = mail.post(ZP.at[half], ZP.at[half], partner)
    for copy in above:
        copy.wait_recv()

    for copy in second:
        copy.wait_recv()
    third = []
    for d in (2, 1, 3):
        third.append(
            mail.post(WR.at[0:2, core, :, y], WR.at[0:2, core, :, y], near(0, d, 0))
        )
        third.append(
            mail.post(WR.at[2:4, core, x], WR.at[2:4, core, x], near(d, 0, 0))
        )
    hand = [
        mail.post(WR.at[0:2, core, :, y], WR.at[0:2, core, :, y], partner),
        mail.post(WR.at[2:4, core, x], WR.at[2:4, core, x], partner),
    ]

    zrow = 13 - 13 * zhi
    relay.wait_recv()

    def cap(i, carry):
        G[pl.ds((i + 1) * 416 + 16 + zrow, 24, stride=16), :] = ZP[i].astype(F32)
        return carry

    lax.fori_loop(0, 24, cap, 0)
    for s in (0, 1):
        G[pl.ds(s * 25 * 416 + 16 + zrow, 24, stride=16), :] = ZX[s].astype(F32)
        G[pl.ds(416 + s * 25 * 16 + zrow, 24, stride=416), :] = ZY[s].astype(F32)
    for sx in (0, 1):
        for sy in (0, 1):
            strip_rows = ZC[sx * 2 + sy].astype(F32)
            pick = 0 if sx else 23
            G[pl.ds(sx * 25 * 416 + sy * 25 * 16 + zrow, 1), :] = strip_rows[pick : pick + 1]

    second_copy = core == 1
    gain = jnp.where(second_copy, scale[...], 1.0)
    offset = jnp.where(second_copy, shift[...], 0.0)
    level = lax.broadcasted_iota(jnp.int32, (16, 128), 0)

    def fill(i, carry):
        inside = (i > 0) | (x > 0)
        inside = inside & ((i < 25) | (x < 3))
        for j in range(26):
            ok = inside
            if j == 0:
                ok = ok & (y > 0)
            if j == 25:
                ok = ok & (y < 3)
            lowest = jnp.where(ok, 1 - zhi, 100)
            w = G[pl.ds(pl.multiple_of(i * 416 + j * 16, 16), 16), :] * gain + offset
            w = jnp.where((level >= lowest) & (level <= 13 - zhi), w, 0.0)
            at = pl.ds(pl.multiple_of(i * 16, 16), 16)
            lanes = slice(j * 128, j * 128 + 128)
            A[0, at, lanes] = w.astype(BF16)
            A[1, at, lanes] = pltpu.roll(w, 15, 0).astype(BF16)
            A[2, at, lanes] = pltpu.roll(w, 14, 0).astype(BF16)
        return carry

    lax.fori_loop(0, 26, fill, 0)

    bias = jnp.concatenate([fbias[...], fbias[...]], axis=1)

    def conv(cy, carry):
        for pair in range(2):
            start = pl.multiple_of((cy * 4 + pair * 2) * 128, 256)
            total = None
            for dx in range(3):
                for dz in range(3):
                    term = jnp.dot(
                        A[dz, dx * 16 : dx * 16 + 384, pl.ds(start, 512)],
                        WZ[dx * 3 + dz],
                        preferred_element_type=F32,
                    )
                    total = term if total is None else total + term
            value = silu(total + bias)
            for i in range(24):
                at = (i % 4 * 6 + i // 4) * 16
                for o in range(2):
                    H[pair * 2 + o, at : at + 16, :] = value[
                        i * 16 : i * 16 + 16, o * 128 : o * 128 + 128
                    ]
        for yo in range(4):
            for xo in range(4):
                for zo in range(4):
                    part = xo * 16 + yo * 4 + zo
                    HID[pl.ds(pl.multiple_of(cy * 32, 32), 32), part * 128 : part * 128 + 128] = H[
                        yo, pl.ds(xo * 96 + zo, 32, stride=4), :
                    ].astype(BF16)
        return carry

    lax.fori_loop(0, 6, conv, 0)

    for n, d in enumerate((2, 1, 3)):
        third[2 * n].wait_recv()
        y_from = (y + 4 - d) % 4
        hand.append(mail.post(WR.at[0:2, core, :, y_from], WR.at[0:2, core, :, y_from], partner))
        third[2 * n + 1].wait_recv()
        x_from = (x + 4 - d) % 4
        hand.append(mail.post(WR.at[2:4, core, x_from], WR.at[2:4, core, x_from], partner))
    for copy in hand:
        copy.wait_recv()

    def regroup(i, carry):
        z = i // 8
        k = i // 4 % 2
        block = pl.ds(pl.multiple_of(i % 4 * 16, 16), 16)
        rows = WR[z, k, :, :, block, :].reshape(256, 256)
        turned = jnp.dot(PM[...], rows, preferred_element_type=F32).astype(BF16)
        WP[block, pl.ds(pl.multiple_of((z * 2 + k) * 16, 16), 16), :] = turned.reshape(16, 16, 256)
        return carry

    lax.fori_loop(0, 32, regroup, 0)

    def project(i, total):
        lanes = pl.ds(pl.multiple_of(i * 1024, 1024), 1024)
        rows = WP[pl.ds(i * 8, 8)].reshape(1024, 256)
        return total + jnp.dot(HID[:, lanes], rows, preferred_element_type=F32)

    total = lax.fori_loop(0, 8, project, jnp.zeros((192, 256), F32))
    total = total + pbias[:, pl.ds(pl.multiple_of(zlo * 256, 256), 256)]
    total = total.astype(BF16).astype(F32)
    for h in range(2):
        CF[h] = total[:, h * 128 : h * 128 + 128]

    mine = FR.at[core]
    for cz in range(3):
        for cx in range(6):
            for h in range(2):
                mine[h, cz + 1, (cx + 1) * 8 + 1 : (cx + 1) * 8 + 7, :] = CF[
                    h, pl.ds(cx * 4 + cz, 6, stride=32), :
                ]
    for cz in range(3):
        for h in range(2):
            YB[0, h, cz] = mine[h, cz + 1, pl.ds(1, 8, stride=8), :]
            YB[1, h, cz] = mine[h, cz + 1, pl.ds(6, 8, stride=8), :]
    top = 2 - 2 * zhi
    wide = {-1: 6, 1: 1}
    around = []
    around.append(mail.post(mine.at[:, top + 1, 8:56], CZ, near(0, 0, 1)))
    for sx in SIDES:
        for sy in SIDES:
            around.append(
                mail.post(YB.at[strip[sy], :, top], CZC.at[slot[sx] * 2 + slot[sy]], near(-sx, -sy, 1))
            )
    for s in SIDES:
        column = slice(wide[s] * 8, wide[s] * 8 + 8)
        around.append(mail.post(mine.at[:, top + 1, column], CZX.at[slot[s]], near(-s, 0, 1)))
        around.append(mail.post(YB.at[strip[s], :, top], CZY.at[slot[s]], near(0, -s, 1)))
    for sx in SIDES:
        for sy in SIDES:
            around.append(
                mail.post(YB.at[strip[sy]], CC.at[slot[sx] * 2 + slot[sy]], near(-sx, -sy, 0))
            )
    for s in SIDES:
        column = slice(wide[s] * 8, wide[s] * 8 + 8)
        around.append(mail.post(mine.at[:, 1:4, column], CX.at[slot[s]], near(-s, 0, 0)))
        around.append(mail.post(YB.at[strip[s]], CY.at[slot[s]], near(0, -s, 0)))
    for copy in around:
        copy.wait_send()
    for copy in around:
        copy.wait_recv()

    place8 = lax.broadcasted_iota(jnp.int32, (8, 128), 0)
    x_ok = (x > 0, x < 3)
    y_ok = (y > 0, y < 3)

    def frame(h, cz, in_x, in_y, in_corner):
        for s in (0, 1):
            mine[h, cz, s * 56 : s * 56 + 8, :] = jnp.where(x_ok[s], in_x[s], 0.0)
        for s in (0, 1):
            low = jnp.broadcast_to(in_corner[s][6:7], (8, 128))
            high = jnp.broadcast_to(in_corner[2 + s][1:2], (8, 128))
            value = jnp.where(place8 == 0, jnp.where(x_ok[0], low, 0.0), in_y[s])
            value = jnp.where(place8 == 7, jnp.where(x_ok[1], high, 0.0), value)
            mine[h, cz, pl.ds(s * 7, 8, stride=8), :] = jnp.where(y_ok[s], value, 0.0)

    lid = 4 - 4 * zhi
    for h in range(2):
        for cz in range(3):
            frame(
                h,
                cz + 1,
                [CX[s, h, cz] for s in (0, 1)],
                [CY[s, h, cz] for s in (0, 1)],
                [CC[s, h, cz] for s in range(4)],
            )
        mine[h, 4 * zhi] = jnp.zeros((64, 128), F32)
        mine[h, lid, 8:56, :] = CZ[h]
        frame(
            h,
            lid,
            [CZX[s, h] for s in (0, 1)],
            [CZY[s, h] for s in (0, 1)],
            [CZC[s, h] for s in range(4)],
        )

    trade = mail.post(FR.at[core], FR.at[core], partner)
    trade.wait_recv()

    def stack(i, carry):
        c = i // 5
        z = i % 5
        for h in range(2):
            w = FR[c, h, z]
            for dy in range(3):
                turned = w if dy == 0 else pltpu.roll(w, 64 - dy, 0)
                for dx in range(3):
                    FB[dx * 3 + dy, c, z, :, h * 128 : h * 128 + 128] = turned[
                        dx * 8 : dx * 8 + 48
                    ].astype(BF16)
        return carry

    lax.fori_loop(0, 10, stack, 0)

    for copy in own_b:
        copy.wait()
    for copy in swap_b:
        copy.wait_recv()
    T[...] = jnp.zeros((288, 512), F32)

    def bottle(i, carry):
        total = T[...]
        for dz in range(3):
            rows = FB[i, :, dz : dz + 3].reshape(288, 256)
            total = total + jnp.dot(rows, BW[i * 3 + dz], preferred_element_type=F32)
        T[...] = total
        return carry

    lax.fori_loop(0, 9, bottle, 0)

    for c in range(2):
        for g in range(18):
            at = (c * 18 + g) * 8
            for z in range(4):
                TS[z, c, g * 6 : g * 6 + 6, :] = T[at : at + 6, z * 128 : z * 128 + 128]

    gather = []
    for d in (2, 1, 3):
        z = (zlo + d) % 4
        gather.append(mail.post(TS.at[z], RB.at[d - 1], device_at(z, core, x, y, zhi)))
    for copy in gather:
        copy.wait_recv()
    lane = pl.ds(pl.multiple_of((zlo * 2 + core) * 128, 128), 128)
    result = []
    for c in range(2):
        value = TS[zlo, c] + RB[0, c] + RB[1, c] + RB[2, c]
        result.append(silu(value + bbias[:, lane]))
    out[...] = (result[0] + guide[0] * (result[1] - result[0])).astype(BF16)

    for copy in mail.all:
        if not any(copy is other for other in around):
            copy.wait_send()


MESSAGES = 80


def shards(lat, scale, shift, fw, fbias, pw, pbias, bw, bbias, guide):
    anywhere = pl.BlockSpec(memory_space=pl.ANY)
    vmem = pl.BlockSpec(memory_space=pltpu.VMEM)
    scratch = [
        pltpu.VMEM((24, 24, 12, 128), BF16),
        pltpu.VMEM((26 * 416, 128), F32),
        pltpu.VMEM((3, 416, 26 * 128), BF16),
        pltpu.VMEM((3, 3, 3, 128, 128), BF16),
        pltpu.VMEM((9, 512, 256), BF16),
        pltpu.VMEM((4, 416, 128), F32),
        pltpu.VMEM((192, 8192), BF16),
        pltpu.VMEM((4, 2, 4, 4, 64, 256), BF16),
        pltpu.VMEM((64, 128, 256), BF16),
        pltpu.VMEM((256, 256), BF16),
        pltpu.VMEM((27, 256, 512), BF16),
        pltpu.VMEM((2, 192, 128), F32),
        pltpu.VMEM((2, 2, 5, 64, 128), F32),
        pltpu.VMEM((9, 2, 5, 48, 256), BF16),
        pltpu.VMEM((288, 512), F32),
        pltpu.VMEM((4, 2, 108, 128), F32),
        pltpu.VMEM((3, 2, 108, 128), F32),
        pltpu.VMEM((2, 2, 3, 8, 128), F32),
        pltpu.VMEM((2, 24, 12, 128), BF16),
        pltpu.VMEM((2, 24, 12, 128), BF16),
        pltpu.VMEM((4, 12, 128), BF16),
        pltpu.VMEM((24, 24, 128), BF16),
        pltpu.VMEM((2, 24, 128), BF16),
        pltpu.VMEM((24, 24, 128), BF16),
        pltpu.VMEM((2, 24, 128), BF16),
        pltpu.VMEM((2, 24, 128), BF16),
        pltpu.VMEM((4, 24, 128), BF16),
        pltpu.VMEM((2, 2, 3, 8, 128), F32),
        pltpu.VMEM((2, 2, 3, 8, 128), F32),
        pltpu.VMEM((4, 2, 3, 8, 128), F32),
        pltpu.VMEM((2, 48, 128), F32),
        pltpu.VMEM((2, 2, 8, 128), F32),
        pltpu.VMEM((2, 2, 8, 128), F32),
        pltpu.VMEM((4, 2, 8, 128), F32),
        pltpu.SemaphoreType.DMA((8,)),
        pltpu.SemaphoreType.DMA((MESSAGES,)),
        pltpu.SemaphoreType.DMA((MESSAGES,)),
    ]
    rows = pl.pallas_call(
        kernel,
        out_shape=jax.ShapeDtypeStruct((108, 128), BF16),
        in_specs=[
            anywhere, vmem, vmem, anywhere, vmem, anywhere, vmem, anywhere, vmem,
            pl.BlockSpec(memory_space=pltpu.SMEM),
        ],
        out_specs=vmem,
        scratch_shapes=scratch,
        compiler_params=pltpu.CompilerParams(
            collective_id=0, has_side_effects=True, vmem_limit_bytes=67043328
        ),
        name="denoise",
    )(
        lat,
        scale.reshape(1, -1),
        shift.reshape(1, -1),
        fw,
        fbias.reshape(1, -1),
        pw,
        pbias.reshape(1, -1),
        bw,
        bbias.reshape(1, -1),
        guide,
    )
    return rows.reshape(3, 6, 6, 128).transpose(1, 2, 0, 3)[None]


def solution(mesh):
    placed = (
        P("region", None, None, None, None),
        P(),
        P(),
        P(),
        P(),
        P(("chan", "region"), None),
        P(),
        P(None, "chan", None),
        P(),
        P(),
    )
    return jax.shard_map(
        shards,
        mesh=mesh,
        in_specs=placed,
        out_specs=P("region", None, None, None, "chan"),
        check_vma=False,
    )
```

```python
import functools

import jax
import jax.numpy as jnp
from jax import lax
from jax.experimental import pallas as pl
from jax.experimental.pallas import tpu as pltpu
from jax.sharding import PartitionSpec as P

F32 = jnp.float32
BF16 = jnp.bfloat16
SIDES = (-1, 1)


def place_of():
    c = lax.axis_index("chan")
    r = lax.axis_index("region")
    return c // 2, c % 2, r // 8, r // 2 % 4, r % 2


def device_at(zlo, core, x, y, zhi):
    return (zlo * 2 + core, (x * 4 + y) * 2 + zhi)


class Parcel:
    def __init__(self, copy):
        self.copy, self.sent, self.received = copy, False, False

    def wait_send(self):
        if not self.sent:
            self.copy.wait_send()
        self.sent = True

    def wait_recv(self):
        if not self.received:
            self.copy.wait_recv()
        self.received = True


class Mail:
    def __init__(self, send, recv):
        self.send, self.recv = send, recv
        self.all = []

    def post(self, src, dst, target):
        copy = pltpu.make_async_remote_copy(
            src_ref=src,
            dst_ref=dst,
            send_sem=self.send.at[len(self.all)],
            recv_sem=self.recv.at[len(self.all)],
            device_id=target,
            device_id_type=pl.DeviceIdType.MESH,
        )
        copy.start()
        self.all.append(Parcel(copy))
        return self.all[-1]


def silu(v):
    return v / (1.0 + jnp.exp(-v))


def kernel(
    lat, scale, shift, fw, fbias, pw, pbias, bw, bbias, guide,
    out,
    L, G, A, FW, WZ, H, HID, WR, WP, PM, BW, CF, FR, FB, FZ, ZF, T, TS, TB, RB, OF, YB, ZB, YZ, XZ,
    HX, HY, HC, YS, CS, HZ, HZX, HZY, HZC,
    CX, CY, CC, CZ, CZX, CZY, CZC,
    lsem, ssem, rsem,
):
    zlo, core, x, y, zhi = place_of()
    mail = Mail(ssem, rsem)

    def near(sx, sy, sz):
        return device_at(zlo, core, (x + sx) % 4, (y + sy) % 4, (zhi + sz) % 2)

    def line(dz):
        z = (zhi * 4 + zlo + dz) % 8
        return device_at(z % 4, core, x, y, z // 4)

    partner = device_at(zlo, 1 - core, x, y, zhi)

    barrier = pltpu.get_barrier_semaphore()
    friends = [near(sx, sy, 0) for sx in (-1, 0, 1) for sy in (-1, 0, 1) if sx or sy]
    friends += [near(sx, sy, 1) for sx in (-1, 0, 1) for sy in (-1, 0, 1)]
    friends += [near(2, 0, 0), near(0, 2, 0)]
    friends += [line(d) for d in (1, 2, 3, 5, 6, 7)]
    friends += [partner]
    for friend in friends:
        pl.semaphore_signal(barrier, inc=1, device_id=friend, device_id_type=pl.DeviceIdType.MESH)

    loads = []

    def load(src, dst):
        copy = pltpu.make_async_copy(src, dst, lsem.at[len(loads)])
        copy.start()
        loads.append(copy)
        return copy

    load_lat = [load(lat.at[0, i * 6 : i * 6 + 6], L.at[i * 6 : i * 6 + 6]) for i in range(4)]
    load_fw = load(fw, FW)
    own_w = load(
        pw.at[:, pl.ds(pl.multiple_of(zlo * 256, 256), 256)],
        WR.at[zlo, core, x, y, pl.ds(pl.multiple_of(zhi * 32, 32), 32)],
    )
    pl.semaphore_wait(barrier, len(friends))

    rows_here = pl.ds(pl.multiple_of(zhi * 32, 32), 32)
    first = []
    for d in (4, 3, 5, 2, 6, 1, 7):
        z_there = (zhi * 4 + zlo + d) % 8 % 4
        first.append(
            mail.post(
                pw.at[:, pl.ds(pl.multiple_of(z_there * 256, 256), 256)],
                WR.at[zlo, core, x, y, rows_here],
                line(d),
            )
        )

    edge = {-1: 23, 1: 0}
    slot = {-1: 0, 1: 1}
    strip = {-1: 1, 1: 0}
    end = 11 - 11 * zhi
    fine = []
    for s in SIDES:
        fine.append(mail.post(lat.at[0, edge[s]], HX.at[slot[s]], near(-s, 0, 0)))
    half = pl.ds(pl.multiple_of(core * 12, 12), 12)
    face = mail.post(lat.at[0, half, end], HZ.at[half], near(0, 0, 1))
    above = [mail.post(lat.at[0, edge[s], end], HZX.at[slot[s]], near(-s, 0, 1)) for s in SIDES]

    gain = jnp.where(core == 1, scale[...], 1.0)
    offset = jnp.where(core == 1, shift[...], 0.0)

    def condition(values):
        return (values.astype(F32) * gain + offset).astype(BF16).astype(F32)

    def widen(i, carry):
        for z in range(12):
            at = pl.multiple_of(((z + 1) * 26 + i + 1) * 40 + 8, 8)
            G[pl.ds(at, 24), :] = condition(L[i, z])
        return carry

    for i in range(4):
        load_lat[i].wait()
        lax.fori_loop(i * 6, i * 6 + 6, widen, 0)

    def side(z, carry):
        at = ((z + 1) * 26 + 1) * 40 + 8
        YS[0, z] = G[pl.ds(at, 24, stride=40), :].astype(BF16)
        YS[1, z] = G[pl.ds(at + 23, 24, stride=40), :].astype(BF16)
        return carry

    lax.fori_loop(0, 12, side, 0)
    for sx in (0, 1):
        for sy in (0, 1):
            at = (26 + 1 + 23 * sx) * 40 + 8 + 23 * sy
            CS[sx * 2 + sy] = G[pl.ds(at, 12, stride=1040), :].astype(BF16)

    for s in SIDES:
        fine.append(mail.post(YS.at[strip[s]], HY.at[slot[s]], near(0, -s, 0)))
    for sx in SIDES:
        for sy in SIDES:
            fine.append(
                mail.post(
                    CS.at[strip[sx] * 2 + strip[sy]],
                    HC.at[slot[sx] * 2 + slot[sy]],
                    near(-sx, -sy, 0),
                )
            )
    for s in SIDES:
        above.append(mail.post(YS.at[strip[s], end], HZY.at[slot[s]], near(0, -s, 1)))
    for sx in SIDES:
        for sy in SIDES:
            above.append(
                mail.post(
                    CS.at[strip[sx] * 2 + strip[sy]],
                    HZC.at[slot[sx] * 2 + slot[sy]],
                    near(-sx, -sy, 1),
                )
            )

    load_fw.wait()
    from_ch = lax.broadcasted_iota(jnp.int32, (128, 128), 0)
    to_ch = lax.broadcasted_iota(jnp.int32, (128, 128), 1)
    group, member = to_ch >> 4, to_ch & 15
    low_ch = (member >> 2) * 16 + (member & 3) * 4 + group
    high_ch = 64 + (member >> 2) * 16 + (group - 4) * 4 + (member & 3)
    order = from_ch == jnp.where(group < 4, low_ch, high_ch)
    order16 = jnp.where(order, 1.0, 0.0).astype(BF16)

    def arrange(i, carry):
        WZ[i, 3 * 128 : 4 * 128, 0:128] = jnp.zeros((128, 128), BF16)
        WZ[i, 0:128, 128:256] = jnp.zeros((128, 128), BF16)
        for dz in range(3):
            tap = jnp.dot(FW[i * 3 + dz], order16, preferred_element_type=F32).astype(BF16)
            for o in range(2):
                at = (dz + o) * 128
                WZ[i, at : at + 128, o * 128 : o * 128 + 128] = tap
        return carry

    lax.fori_loop(0, 9, arrange, 0)
    bias = jnp.dot(
        jnp.broadcast_to(fbias[...], (8, 128)),
        jnp.where(order, 1.0, 0.0),
        preferred_element_type=F32,
        precision=lax.Precision.HIGHEST,
    )[0:1]
    bias = jnp.concatenate([bias, bias], axis=1)
    row = lax.broadcasted_iota(jnp.int32, (256, 256), 0)
    col = lax.broadcasted_iota(jnp.int32, (256, 256), 1)
    PM[...] = jnp.where(col == (row & 15) * 16 + (row >> 4), 1.0, 0.0).astype(BF16)
    H[:, 576:624, :] = jnp.zeros((4, 48, 128), F32)

    own_w.wait()
    for copy in first:
        copy.wait_recv()
    span = (slice(0, 2), slice(2, 4))
    low_x, high_y, low_y, high_x = {}, {}, {}, {}

    def low(x_at, y_at):
        return WR.at[span[0], core, x_at, y_at]

    def high(x_at, y_at):
        return WR.at[span[1], core, x_at, y_at]

    for d in (2, 1, 3):
        low_x[d] = mail.post(low(x, y), low(x, y), near(d, 0, 0))
        high_y[d] = mail.post(high(x, y), high(x, y), near(0, d, 0))
    for d in (2, 1, 3):
        low_y[0, d] = mail.post(low(x, y), low(x, y), near(0, d, 0))
        high_x[0, d] = mail.post(high(x, y), high(x, y), near(d, 0, 0))

    for copy in fine:
        copy.wait_recv()
    x_ok = (x > 0, x < 3)
    y_ok = (y > 0, y < 3)

    def border(z, carry):
        base = (z + 1) * 1040
        for s in (0, 1):
            G[pl.ds(pl.multiple_of(base + s * 1000 + 8, 8), 24), :] = jnp.where(
                x_ok[s], condition(HX[s, z]), 0.0
            )
            G[pl.ds(base + 40 + 7 + s * 25, 24, stride=40), :] = jnp.where(
                y_ok[s], HY[s, z].astype(F32), 0.0
            )
        return carry

    lax.fori_loop(0, 12, border, 0)
    for sx in (0, 1):
        for sy in (0, 1):
            G[pl.ds(1040 + sx * 1000 + 7 + sy * 25, 12, stride=1040), :] = jnp.where(
                x_ok[sx] & y_ok[sy], HC[sx * 2 + sy].astype(F32), 0.0
            )

    def fill(z):
        lanes = pl.ds(pl.multiple_of(z * 128, 128), 128)
        for parity in range(2):
            for m in range(13 - parity):
                at = z * 1040 + (2 * m + parity) * 40 + 7
                for dy in range(3):
                    pair = jnp.concatenate(
                        [G[pl.ds(at + dy, 24), :], G[pl.ds(at + dy + 40, 24), :]], axis=0
                    )
                    A[parity, dy, m * 48 : m * 48 + 48, lanes] = pair.astype(BF16)

    def inner(z, carry):
        fill(z + 1)
        return carry

    lax.fori_loop(0, 12, inner, 0)

    def conv(cz):
        for pair in range(2):
            start = pl.multiple_of((cz * 2 + pair) * 256, 256)
            total = None
            for dx in range(3):
                for dy in range(3):
                    first_row = dx // 2 * 48
                    term = jnp.dot(
                        A[dx % 2, dy, first_row : first_row + 576, pl.ds(start, 512)],
                        WZ[dx * 3 + dy],
                        preferred_element_type=F32,
                    )
                    total = term if total is None else total + term
            value = silu(total + bias)
            for i in range(24):
                at = (i % 4 * 6 + i // 4) * 24
                for o in range(2):
                    H[pair * 2 + o, at : at + 24, :] = value[
                        i * 24 : i * 24 + 24, o * 128 : o * 128 + 128
                    ]
        for zo in range(4):
            for xo in range(4):
                for yo in range(4):
                    part = xo * 16 + yo * 4 + zo
                    HID[pl.ds(pl.multiple_of(cz * 48, 16), 48), part * 128 : part * 128 + 128] = H[
                        zo, pl.ds(xo * 144 + yo, 48, stride=4), :
                    ].astype(BF16)

    for e in (1, 3, 2):
        low_x[e].wait_recv()
        x_from = (x + 4 - e) % 4
        for d in (2, 1, 3):
            low_y[e, d] = mail.post(low(x_from, y), low(x_from, y), near(0, d, 0))
        high_y[e].wait_recv()
        y_from = (y + 4 - e) % 4
        for d in (2, 1, 3):
            high_x[e, d] = mail.post(high(x, y_from), high(x, y_from), near(d, 0, 0))
    hand = {
        (0, 0): mail.post(low(slice(None), y), low(slice(None), y), partner),
        (1, 0): mail.post(high(x, slice(None)), high(x, slice(None)), partner),
    }

    own_b = [
        load(
            bw.at[:, :, pl.ds(pl.multiple_of((2 * z + core) * 128, 128), 128)],
            BW.at[:, pl.ds(pl.multiple_of(core * 128, 128), 128), z * 128 : z * 128 + 128],
        )
        for z in range(4)
    ]
    swap_b = [
        mail.post(
            bw.at[:, :, pl.ds(pl.multiple_of((2 * z + 1 - core) * 128, 128), 128)],
            BW.at[:, pl.ds(pl.multiple_of(core * 128, 128), 128), z * 128 : z * 128 + 128],
            partner,
        )
        for z in range(4)
    ]

    def far(i, carry):
        conv(i + zhi)
        return carry

    near_plane = 13 - 13 * zhi

    def blank(i, carry):
        G[pl.ds(pl.multiple_of(zrow0 + i * 40, 8), 40), :] = jnp.zeros((40, 128), F32)
        return carry

    zrow0 = (13 - near_plane) * 1040
    lax.fori_loop(0, 26, blank, 0)
    fill(13 - near_plane)
    lax.fori_loop(0, 2, far, 0)

    face.wait_recv()
    relay = mail.post(HZ.at[half], HZ.at[half], partner)
    for copy in above:
        copy.wait_recv()
    relay.wait_recv()
    base = near_plane * 1040

    def cap(i, carry):
        G[pl.ds(pl.multiple_of(base + (i + 1) * 40 + 8, 8), 24), :] = condition(HZ[i])
        return carry

    lax.fori_loop(0, 24, cap, 0)
    for s in (0, 1):
        G[pl.ds(pl.multiple_of(base + s * 1000 + 8, 8), 24), :] = jnp.where(
            x_ok[s], condition(HZX[s]), 0.0
        )
        G[pl.ds(base + 40 + 7 + s * 25, 24, stride=40), :] = jnp.where(
            y_ok[s], HZY[s].astype(F32), 0.0
        )
    for sx in (0, 1):
        for sy in (0, 1):
            there = HZC[sx * 2 + sy].astype(F32)
            cell = jnp.where(zhi == 0, there[0:1], there[11:12])
            G[pl.ds(base + sx * 1000 + 7 + sy * 25, 1), :] = jnp.where(
                x_ok[sx] & y_ok[sy], cell, 0.0
            )
    fill(near_plane)
    conv(2 - 2 * zhi)

    def regroup(upper, at):
        for part in range(4):
            block = slice(part * 16, part * 16 + 16)
            if upper:
                rows = WR[2:4, :, at, :, block, :].reshape(256, 256)
                lane = 64 + at * 16
            else:
                rows = WR[0:2, :, :, at, block, :].reshape(256, 256)
                lane = at * 16
            turned = jnp.dot(PM[...], rows, preferred_element_type=F32).astype(BF16)
            WP[block, pl.ds(pl.multiple_of(lane, 16), 16), :] = turned.reshape(16, 16, 256)

    hand[0, 0].wait_recv()
    regroup(0, y)
    hand[1, 0].wait_recv()
    regroup(1, x)
    turns = (1, 3, 2)
    for d in turns:
        for e in range(4):
            low_y[e, d].wait_recv()
        y_from = (y + 4 - d) % 4
        hand[0, d] = mail.post(low(slice(None), y_from), low(slice(None), y_from), partner)
        for e in range(4):
            high_x[e, d].wait_recv()
        x_from = (x + 4 - d) % 4
        hand[1, d] = mail.post(high(x_from, slice(None)), high(x_from, slice(None)), partner)
        if d != turns[0]:
            before = turns[turns.index(d) - 1]
            hand[0, before].wait_recv()
            regroup(0, (y + 4 - before) % 4)
            hand[1, before].wait_recv()
            regroup(1, (x + 4 - before) % 4)
    before = turns[-1]
    hand[0, before].wait_recv()
    regroup(0, (y + 4 - before) % 4)
    hand[1, before].wait_recv()
    regroup(1, (x + 4 - before) % 4)

    def project(i, total):
        lanes = pl.ds(pl.multiple_of(i * 1024, 1024), 1024)
        rows = WP[pl.ds(i * 8, 8)].reshape(1024, 256)
        return total + jnp.dot(HID[:, lanes], rows, preferred_element_type=F32)

    total = lax.fori_loop(0, 8, project, jnp.zeros((144, 256), F32))
    total = total + pbias[:, pl.ds(pl.multiple_of(zlo * 256, 256), 256)]
    total = total.astype(BF16).astype(F32)
    for h in range(2):
        CF[h] = total[:, h * 128 : h * 128 + 128]

    mine = FR.at[core]
    for cz in range(3):
        for cx in range(6):
            for h in range(2):
                mine[h, cz + 1, (cx + 1) * 8 + 1 : (cx + 1) * 8 + 7, :] = CF[
                    h, cz * 48 + cx * 6 : cz * 48 + cx * 6 + 6, :
                ]
    for cz in range(3):
        for h in range(2):
            YB[0, h, cz] = mine[h, cz + 1, pl.ds(1, 8, stride=8), :]
            YB[1, h, cz] = mine[h, cz + 1, pl.ds(6, 8, stride=8), :]
    top = 2 - 2 * zhi
    wide = {-1: 6, 1: 1}
    ZB[...] = mine[:, top + 1, 8:56].astype(BF16)
    for s in (0, 1):
        YZ[s] = YB[s, :, top].astype(BF16)
    XZ[0] = mine[:, top + 1, 8:16].astype(BF16)
    XZ[1] = mine[:, top + 1, 48:56].astype(BF16)
    around = []
    for sx in SIDES:
        for sy in SIDES:
            around.append(
                mail.post(YB.at[strip[sy]], CC.at[slot[sx] * 2 + slot[sy]], near(-sx, -sy, 0))
            )
    for s in SIDES:
        column = slice(wide[s] * 8, wide[s] * 8 + 8)
        around.append(mail.post(mine.at[:, 1:4, column], CX.at[slot[s]], near(-s, 0, 0)))
        around.append(mail.post(YB.at[strip[s]], CY.at[slot[s]], near(0, -s, 0)))
    beyond = []
    for sx in SIDES:
        for sy in SIDES:
            beyond.append(
                mail.post(YZ.at[strip[sy]], CZC.at[slot[sx] * 2 + slot[sy]], near(-sx, -sy, 1))
            )
    for s in SIDES:
        beyond.append(mail.post(XZ.at[strip[s]], CZX.at[slot[s]], near(-s, 0, 1)))
        beyond.append(mail.post(YZ.at[strip[s]], CZY.at[slot[s]], near(0, -s, 1)))
    beyond.append(mail.post(ZB, CZ, near(0, 0, 1)))
    for copy in around:
        copy.wait_send()
    for copy in around:
        copy.wait_recv()

    place8 = lax.broadcasted_iota(jnp.int32, (8, 128), 0)
    def frame(plane, in_x, in_y, in_corner):
        for s in (0, 1):
            plane[s * 56 : s * 56 + 8, :] = jnp.where(x_ok[s], in_x[s], 0.0)
        for s in (0, 1):
            low_row = jnp.broadcast_to(in_corner[s][6:7], (8, 128))
            high_row = jnp.broadcast_to(in_corner[2 + s][1:2], (8, 128))
            value = jnp.where(place8 == 0, jnp.where(x_ok[0], low_row, 0.0), in_y[s])
            value = jnp.where(place8 == 7, jnp.where(x_ok[1], high_row, 0.0), value)
            plane[pl.ds(s * 7, 8, stride=8), :] = jnp.where(y_ok[s], value, 0.0)

    for h in range(2):
        for cz in range(3):
            frame(
                mine.at[h, cz + 1],
                [CX[s, h, cz] for s in (0, 1)],
                [CY[s, h, cz] for s in (0, 1)],
                [CC[s, h, cz] for s in range(4)],
            )
    trade = mail.post(mine.at[:, 1:4], mine.at[:, 1:4], partner)

    def spread(w, put):
        for dy in range(3):
            turned = w if dy == 0 else pltpu.roll(w, 64 - dy, 0)
            for dx in range(3):
                put(dx * 3 + dy, turned[dx * 8 : dx * 8 + 48].astype(BF16))

    def lay(c, z, h):
        def put(i, rows):
            FB[i, c, z, :, h * 128 : h * 128 + 128] = rows

        spread(FR[c, h, z], put)

    def blank_ends(i, carry):
        for c in range(2):
            for z in (0, 4):
                FB[i, c, z] = jnp.zeros((48, 256), BF16)
        return carry

    lax.fori_loop(0, 9, blank_ends, 0)

    def stack_own(i, carry):
        for h in range(2):
            lay(core, i + 1, h)
        return carry

    lax.fori_loop(0, 3, stack_own, 0)
    trade.wait_recv()

    def stack_other(i, carry):
        for h in range(2):
            lay(1 - core, i + 1, h)
        return carry

    lax.fori_loop(0, 3, stack_other, 0)

    for copy in own_b:
        copy.wait()
    for copy in swap_b:
        copy.wait_recv()
    first_half = 1 - zlo // 2

    def bottle(step, carry):
        n = pl.ds(pl.multiple_of(((first_half + step) % 2) * 256, 256), 256)
        T[step] = jnp.zeros((288, 256), F32)

        def taps(i, carry):
            total = T[step]
            for dz in range(3):
                rows = FB[i, :, dz : dz + 3].reshape(288, 256)
                total = total + jnp.dot(rows, BW[i * 3 + dz, :, n], preferred_element_type=F32)
            T[step] = total
            return carry

        return lax.fori_loop(0, 9, taps, carry)

    lax.fori_loop(0, 2, bottle, 0)

    for copy in beyond:
        copy.wait_recv()
    for h in range(2):
        ZF[core, h, 8:56, :] = CZ[h].astype(F32)
        frame(
            ZF.at[core, h],
            [CZX[s, h].astype(F32) for s in (0, 1)],
            [CZY[s, h].astype(F32) for s in (0, 1)],
            [CZC[s, h].astype(F32) for s in range(4)],
        )
    trade_z = mail.post(ZF.at[core], ZF.at[core], partner)
    trade_z.wait_recv()
    for c in range(2):
        for h in range(2):

            def put(i, rows, c=c, h=h):
                FZ[i, c * 48 : c * 48 + 48, h * 128 : h * 128 + 128] = rows

            spread(ZF[c, h], put)

    gather = []
    for step in range(2):
        half_at = (first_half + step) % 2
        n = pl.ds(pl.multiple_of(half_at * 256, 256), 256)

        def cap_taps(i, total):
            return total + jnp.dot(FZ[i], BW[i * 3 + top, :, n], preferred_element_type=F32)

        extra = lax.fori_loop(0, 9, cap_taps, jnp.zeros((96, 256), F32))
        for c in range(2):
            at = pl.ds(pl.multiple_of(c * 144 + top * 48, 16), 48)
            T[step, at, :] = T[step, at, :] + extra[c * 48 : c * 48 + 48]
        for c in range(2):
            for g in range(18):
                at = (c * 18 + g) * 8
                for j in range(2):
                    TS[half_at * 2 + j, c, g * 6 : g * 6 + 6, :] = T[
                        step, at : at + 6, j * 128 : j * 128 + 128
                    ]
        if step == 0:
            targets = [half_at * 2 + (zlo + j) % 2 for j in range(2)]
        else:
            targets = [half_at * 2 + (zlo + 1) % 2]
        for z in targets:
            TB[len(gather)] = TS[z].astype(TB.dtype)
            gather.append(
                mail.post(
                    TB.at[len(gather)], RB.at[len(gather)], device_at(z, core, x, y, zhi)
                )
            )
    for copy in gather:
        copy.wait_recv()
    lane = pl.ds(pl.multiple_of((zlo * 2 + core) * 128, 128), 128)
    result = []
    for c in range(2):
        value = TS[zlo, c]
        for j in range(3):
            value = value + RB[j, c].astype(F32)
        result.append(silu(value + bbias[:, lane]))
    OF[...] = result[0] + guide[0] * (result[1] - result[0])
    for g in range(18):
        out[g // 6, g % 6, 0:6, :] = OF[g * 6 : g * 6 + 6, :].astype(BF16)
    for g in range(18):
        out[g // 6, g % 6, 6:8, :] = jnp.zeros((2, 128), BF16)

    for copy in mail.all:
        copy.wait_send()


MESSAGES = 120


def shards(lat, scale, shift, fw, fbias, pw, pbias, bw, bbias, guide):
    anywhere = pl.BlockSpec(memory_space=pl.ANY)
    vmem = pl.BlockSpec(memory_space=pltpu.VMEM)
    scratch = [
        pltpu.VMEM((24, 12, 24, 128), BF16),
        pltpu.VMEM((14 * 1040, 128), F32),
        pltpu.VMEM((2, 3, 624, 14 * 128), BF16),
        pltpu.VMEM((27, 128, 128), BF16),
        pltpu.VMEM((9, 512, 256), BF16),
        pltpu.VMEM((4, 624, 128), F32),
        pltpu.VMEM((144, 8192), BF16),
        pltpu.VMEM((4, 2, 4, 4, 64, 256), BF16),
        pltpu.VMEM((64, 128, 256), BF16),
        pltpu.VMEM((256, 256), BF16),
        pltpu.VMEM((27, 256, 512), BF16),
        pltpu.VMEM((2, 144, 128), F32),
        pltpu.VMEM((2, 2, 5, 64, 128), F32),
        pltpu.VMEM((9, 2, 5, 48, 256), BF16),
        pltpu.VMEM((9, 96, 256), BF16),
        pltpu.VMEM((2, 2, 64, 128), F32),
        pltpu.VMEM((2, 288, 256), F32),
        pltpu.VMEM((4, 2, 108, 128), F32),
        pltpu.VMEM((3, 2, 108, 128), BF16),
        pltpu.VMEM((3, 2, 108, 128), BF16),
        pltpu.VMEM((108, 128), F32),
        pltpu.VMEM((2, 2, 3, 8, 128), F32),
        pltpu.VMEM((2, 48, 128), BF16),
        pltpu.VMEM((2, 2, 8, 128), BF16),
        pltpu.VMEM((2, 2, 8, 128), BF16),
        pltpu.VMEM((2, 12, 24, 128), BF16),
        pltpu.VMEM((2, 12, 24, 128), BF16),
        pltpu.VMEM((4, 12, 128), BF16),
        pltpu.VMEM((2, 12, 24, 128), BF16),
        pltpu.VMEM((4, 12, 128), BF16),
        pltpu.VMEM((24, 24, 128), BF16),
        pltpu.VMEM((2, 24, 128), BF16),
        pltpu.VMEM((2, 24, 128), BF16),
        pltpu.VMEM((4, 12, 128), BF16),
        pltpu.VMEM((2, 2, 3, 8, 128), F32),
        pltpu.VMEM((2, 2, 3, 8, 128), F32),
        pltpu.VMEM((4, 2, 3, 8, 128), F32),
        pltpu.VMEM((2, 48, 128), BF16),
        pltpu.VMEM((2, 2, 8, 128), BF16),
        pltpu.VMEM((2, 2, 8, 128), BF16),
        pltpu.VMEM((4, 2, 8, 128), BF16),
        pltpu.SemaphoreType.DMA((16,)),
        pltpu.SemaphoreType.DMA((MESSAGES,)),
        pltpu.SemaphoreType.DMA((MESSAGES,)),
    ]
    rows = pl.pallas_call(
        kernel,
        out_shape=jax.ShapeDtypeStruct((3, 6, 8, 128), BF16),
        in_specs=[
            anywhere, vmem, vmem, anywhere, vmem, anywhere, vmem, anywhere, vmem,
            pl.BlockSpec(memory_space=pltpu.SMEM),
        ],
        out_specs=vmem,
        scratch_shapes=scratch,
        compiler_params=pltpu.CompilerParams(
            collective_id=0, has_side_effects=True, vmem_limit_bytes=67043328
        ),
        name="denoise",
    )(
        lat.transpose(0, 1, 3, 2, 4),
        scale.reshape(1, -1),
        shift.reshape(1, -1),
        fw.reshape(27, 128, 128),
        fbias.reshape(1, -1),
        pw,
        pbias.reshape(1, -1),
        bw,
        bbias.reshape(1, -1),
        guide,
    )
    return rows[:, :, :6].transpose(1, 2, 0, 3)[None]


def solution(mesh):
    placed = (
        P("region", None, None, None, None),
        P(),
        P(),
        P(),
        P(),
        P(("chan", "region"), None),
        P(),
        P(None, "chan", None),
        P(),
        P(),
    )
    return jax.shard_map(
        shards,
        mesh=mesh,
        in_specs=placed,
        out_specs=P("region", None, None, None, "chan"),
        check_vma=False,
    )
```

```python
import functools

import jax
import jax.numpy as jnp
from jax import lax
from jax.experimental import pallas as pl
from jax.experimental.pallas import tpu as pltpu
from jax.sharding import PartitionSpec as P

F32 = jnp.float32
BF16 = jnp.bfloat16
SIDES = (-1, 1)


def place_of():
    c = lax.axis_index("chan")
    r = lax.axis_index("region")
    return c // 2, c % 2, r // 8, r // 2 % 4, r % 2


def device_at(zlo, core, x, y, zhi):
    return (zlo * 2 + core, (x * 4 + y) * 2 + zhi)


class Parcel:
    def __init__(self, copy):
        self.copy, self.sent, self.received = copy, False, False

    def wait_send(self):
        if not self.sent:
            self.copy.wait_send()
        self.sent = True

    def wait_recv(self):
        if not self.received:
            self.copy.wait_recv()
        self.received = True


class Mail:
    def __init__(self, send, recv):
        self.send, self.recv = send, recv
        self.all = []

    def post(self, src, dst, target):
        copy = pltpu.make_async_remote_copy(
            src_ref=src,
            dst_ref=dst,
            send_sem=self.send.at[len(self.all)],
            recv_sem=self.recv.at[len(self.all)],
            device_id=target,
            device_id_type=pl.DeviceIdType.MESH,
        )
        copy.start()
        self.all.append(Parcel(copy))
        return self.all[-1]


def silu(v):
    return v / (1.0 + jnp.exp(-v))


def kernel(
    lat, scale, shift, fw, fbias, pw, pbias, bw, bbias, guide,
    out,
    L, G, A, FW, WZ, H, HID, WR, WP, PM, BW, CF, FR, FB, FZ, ZF, T, TS, TB, RB, OF, YB, ZB, YZ, XZ,
    HX, HY, HC, YS, CS, HZ, HZX, HZY, HZC,
    CX, CY, CC, CZ, CZX, CZY, CZC,
    lsem, ssem, rsem,
):
    zlo, core, x, y, zhi = place_of()
    mail = Mail(ssem, rsem)

    def near(sx, sy, sz):
        return device_at(zlo, core, (x + sx) % 4, (y + sy) % 4, (zhi + sz) % 2)

    def line(dz):
        z = (zhi * 4 + zlo + dz) % 8
        return device_at(z % 4, core, x, y, z // 4)

    partner = device_at(zlo, 1 - core, x, y, zhi)

    barrier = pltpu.get_barrier_semaphore()
    friends = [near(sx, sy, 0) for sx in (-1, 0, 1) for sy in (-1, 0, 1) if sx or sy]
    friends += [near(sx, sy, 1) for sx in (-1, 0, 1) for sy in (-1, 0, 1)]
    friends += [near(2, 0, 0), near(0, 2, 0)]
    friends += [line(d) for d in (1, 2, 3, 5, 6, 7)]
    friends += [partner]
    for friend in friends:
        pl.semaphore_signal(barrier, inc=1, device_id=friend, device_id_type=pl.DeviceIdType.MESH)

    loads = []

    def load(src, dst):
        copy = pltpu.make_async_copy(src, dst, lsem.at[len(loads)])
        copy.start()
        loads.append(copy)
        return copy

    load_lat = [load(lat.at[0, i * 6 : i * 6 + 6], L.at[i * 6 : i * 6 + 6]) for i in range(4)]
    load_fw = load(fw, FW)
    own_w = load(
        pw.at[:, pl.ds(pl.multiple_of(zlo * 256, 256), 256)],
        WR.at[zlo, core, x, y, pl.ds(pl.multiple_of(zhi * 32, 32), 32)],
    )
    pl.semaphore_wait(barrier, len(friends))

    rows_here = pl.ds(pl.multiple_of(zhi * 32, 32), 32)
    first = []
    for d in (4, 3, 5, 2, 6, 1, 7):
        z_there = (zhi * 4 + zlo + d) % 8 % 4
        first.append(
            mail.post(
                pw.at[:, pl.ds(pl.multiple_of(z_there * 256, 256), 256)],
                WR.at[zlo, core, x, y, rows_here],
                line(d),
            )
        )

    edge = {-1: 23, 1: 0}
    slot = {-1: 0, 1: 1}
    strip = {-1: 1, 1: 0}
    end = 11 - 11 * zhi
    fine = []
    for s in SIDES:
        fine.append(mail.post(lat.at[0, edge[s]], HX.at[slot[s]], near(-s, 0, 0)))

    gain = jnp.where(core == 1, scale[...], 1.0)
    offset = jnp.where(core == 1, shift[...], 0.0)

    def condition(values):
        return (values.astype(F32) * gain + offset).astype(BF16).astype(F32)

    def widen(i, carry):
        for z in range(12):
            at = pl.multiple_of(((z + 1) * 26 + i + 1) * 40 + 8, 8)
            G[pl.ds(at, 24), :] = condition(L[i, z])
        return carry

    for i in range(4):
        load_lat[i].wait()
        lax.fori_loop(i * 6, i * 6 + 6, widen, 0)

    def side(z, carry):
        at = ((z + 1) * 26 + 1) * 40 + 8
        YS[0, z] = G[pl.ds(at, 24, stride=40), :].astype(BF16)
        YS[1, z] = G[pl.ds(at + 23, 24, stride=40), :].astype(BF16)
        return carry

    lax.fori_loop(0, 12, side, 0)
    for sx in (0, 1):
        for sy in (0, 1):
            at = (26 + 1 + 23 * sx) * 40 + 8 + 23 * sy
            CS[sx * 2 + sy] = G[pl.ds(at, 12, stride=1040), :].astype(BF16)

    for s in SIDES:
        fine.append(mail.post(YS.at[strip[s]], HY.at[slot[s]], near(0, -s, 0)))
    for sx in SIDES:
        for sy in SIDES:
            fine.append(
                mail.post(
                    CS.at[strip[sx] * 2 + strip[sy]],
                    HC.at[slot[sx] * 2 + slot[sy]],
                    near(-sx, -sy, 0),
                )
            )
    load_fw.wait()
    from_ch = lax.broadcasted_iota(jnp.int32, (128, 128), 0)
    to_ch = lax.broadcasted_iota(jnp.int32, (128, 128), 1)
    group, member = to_ch >> 4, to_ch & 15
    low_ch = (member >> 2) * 16 + (member & 3) * 4 + group
    high_ch = 64 + (member >> 2) * 16 + (group - 4) * 4 + (member & 3)
    order = from_ch == jnp.where(group < 4, low_ch, high_ch)
    order16 = jnp.where(order, 1.0, 0.0).astype(BF16)

    def arrange(i, carry):
        WZ[i, 3 * 128 : 4 * 128, 0:128] = jnp.zeros((128, 128), BF16)
        WZ[i, 0:128, 128:256] = jnp.zeros((128, 128), BF16)
        for dz in range(3):
            tap = jnp.dot(FW[i * 3 + dz], order16, preferred_element_type=F32).astype(BF16)
            for o in range(2):
                at = (dz + o) * 128
                WZ[i, at : at + 128, o * 128 : o * 128 + 128] = tap
        return carry

    lax.fori_loop(0, 9, arrange, 0)
    bias = jnp.dot(
        jnp.broadcast_to(fbias[...], (8, 128)),
        jnp.where(order, 1.0, 0.0),
        preferred_element_type=F32,
        precision=lax.Precision.HIGHEST,
    )[0:1]
    bias = jnp.concatenate([bias, bias], axis=1)
    row = lax.broadcasted_iota(jnp.int32, (256, 256), 0)
    col = lax.broadcasted_iota(jnp.int32, (256, 256), 1)
    PM[...] = jnp.where(col == (row & 15) * 16 + (row >> 4), 1.0, 0.0).astype(BF16)
    H[:, 576:624, :] = jnp.zeros((4, 48, 128), F32)

    own_w.wait()
    for copy in first:
        copy.wait_recv()

    def low(j, x_at, y_at):
        return WR.at[j, core, x_at % 4, y_at % 4]

    def high(j, x_at, y_at):
        return low(j, x_at, y_at)

    both = {"low": slice(0, 2), "high": slice(2, 4)}
    base_of = {"low": 0, "high": 2}

    class Ring:
        def __init__(self, part, along_x, shift):
            self.part, self.along_x, self.shift = part, along_x, shift
            block = self.at(both[part], 0)
            self.up = mail.post(block, block, self.to(1))
            self.down = mail.post(block, block, self.to(-1))

        def at(self, j, step):
            if self.along_x:
                return low(j, x + 4 + step, y + 4 + self.shift)
            return low(j, x + 4 + self.shift, y + 4 + step)

        def to(self, step):
            return near(4 + step, 0, 0) if self.along_x else near(0, 4 + step, 0)

        def relay(self):
            self.up.wait_recv()
            piece = self.at(base_of[self.part], -1)
            self.up2 = mail.post(piece, piece, self.to(1))
            self.down.wait_recv()
            piece = self.at(base_of[self.part] + 1, 1)
            self.down2 = mail.post(piece, piece, self.to(-1))

        def finish(self):
            self.up2.wait_recv()
            self.down2.wait_recv()

    low_x = Ring("low", True, 0)
    high_y = Ring("high", False, 0)
    low_y = {0: Ring("low", False, 0)}
    high_x = {0: Ring("high", True, 0)}

    half = pl.ds(pl.multiple_of(core * 12, 12), 12)
    face = mail.post(lat.at[0, half, end], HZ.at[half], near(0, 0, 1))
    above = [mail.post(lat.at[0, edge[s], end], HZX.at[slot[s]], near(-s, 0, 1)) for s in SIDES]
    for s in SIDES:
        above.append(mail.post(YS.at[strip[s], end], HZY.at[slot[s]], near(0, -s, 1)))
    for sx in SIDES:
        for sy in SIDES:
            above.append(
                mail.post(
                    CS.at[strip[sx] * 2 + strip[sy]],
                    HZC.at[slot[sx] * 2 + slot[sy]],
                    near(-sx, -sy, 1),
                )
            )

    def step_one():
        low_x.relay()
        high_y.relay()
        for e in (-1, 1):
            low_y[e] = Ring("low", False, e)
            high_x[e] = Ring("high", True, e)
        low_y[0].relay()
        high_x[0].relay()

    def step_two():
        low_x.finish()
        high_y.finish()
        low_y[2] = Ring("low", False, 2)
        high_x[2] = Ring("high", True, 2)

    hand = {}

    def pass_low(step):
        column = WR.at[both["low"], core, :, (y + 4 + step) % 4]
        hand["low", step] = mail.post(column, column, partner)

    def pass_high(step):
        column = WR.at[both["high"], core, (x + 4 + step) % 4]
        hand["high", step] = mail.post(column, column, partner)

    def step_three():
        pass_low(0)
        pass_high(0)
        for e in (-1, 1):
            low_y[e].relay()
            high_x[e].relay()

    def step_four():
        low_y[2].relay()
        high_x[2].relay()
        for e in (-1, 1):
            pass_low(e)
            pass_high(e)

    for copy in fine:
        copy.wait_recv()
    x_ok = (x > 0, x < 3)
    y_ok = (y > 0, y < 3)

    def border(z, carry):
        base = (z + 1) * 1040
        for s in (0, 1):
            G[pl.ds(pl.multiple_of(base + s * 1000 + 8, 8), 24), :] = jnp.where(
                x_ok[s], condition(HX[s, z]), 0.0
            )
            G[pl.ds(base + 40 + 7 + s * 25, 24, stride=40), :] = jnp.where(
                y_ok[s], HY[s, z].astype(F32), 0.0
            )
        return carry

    lax.fori_loop(0, 12, border, 0)
    for sx in (0, 1):
        for sy in (0, 1):
            G[pl.ds(1040 + sx * 1000 + 7 + sy * 25, 12, stride=1040), :] = jnp.where(
                x_ok[sx] & y_ok[sy], HC[sx * 2 + sy].astype(F32), 0.0
            )

    def fill(z):
        lanes = pl.ds(pl.multiple_of(z * 128, 128), 128)
        for parity in range(2):
            for m in range(13 - parity):
                at = z * 1040 + (2 * m + parity) * 40 + 7
                for dy in range(3):
                    pair = jnp.concatenate(
                        [G[pl.ds(at + dy, 24), :], G[pl.ds(at + dy + 40, 24), :]], axis=0
                    )
                    A[parity, dy, m * 48 : m * 48 + 48, lanes] = pair.astype(BF16)

    def inner(z, carry):
        fill(z + 1)
        return carry

    lax.fori_loop(0, 12, inner, 0)

    def conv(cz, pair):
        start = pl.multiple_of((cz * 2 + pair) * 256, 256)
        total = None
        for dx in range(3):
            for dy in range(3):
                first_row = dx // 2 * 48
                term = jnp.dot(
                    A[dx % 2, dy, first_row : first_row + 576, pl.ds(start, 512)],
                    WZ[dx * 3 + dy],
                    preferred_element_type=F32,
                )
                total = term if total is None else total + term
        value = silu(total + bias)
        for i in range(24):
            at = (i % 4 * 6 + i // 4) * 24
            for o in range(2):
                H[pair * 2 + o, at : at + 24, :] = value[
                    i * 24 : i * 24 + 24, o * 128 : o * 128 + 128
                ]

    def collect(cz):
        for zo in range(4):
            for xo in range(4):
                for yo in range(4):
                    part = xo * 16 + yo * 4 + zo
                    HID[pl.ds(pl.multiple_of(cz * 48, 16), 48), part * 128 : part * 128 + 128] = H[
                        zo, pl.ds(xo * 144 + yo, 48, stride=4), :
                    ].astype(BF16)

    step_one()

    own_b = [
        load(
            bw.at[:, :, pl.ds(pl.multiple_of((2 * z + core) * 128, 128), 128)],
            BW.at[:, pl.ds(pl.multiple_of(core * 128, 128), 128), z * 128 : z * 128 + 128],
        )
        for z in range(4)
    ]
    swap_b = [
        mail.post(
            bw.at[:, :, pl.ds(pl.multiple_of((2 * z + 1 - core) * 128, 128), 128)],
            BW.at[:, pl.ds(pl.multiple_of(core * 128, 128), 128), z * 128 : z * 128 + 128],
            partner,
        )
        for z in range(4)
    ]

    near_plane = 13 - 13 * zhi

    def blank(i, carry):
        G[pl.ds(pl.multiple_of(zrow0 + i * 40, 8), 40), :] = jnp.zeros((40, 128), F32)
        return carry

    zrow0 = (13 - near_plane) * 1040
    lax.fori_loop(0, 26, blank, 0)
    fill(13 - near_plane)
    conv(zhi, 0)
    step_two()
    conv(zhi, 1)
    collect(zhi)
    face.wait_recv()
    relay = mail.post(HZ.at[half], HZ.at[half], partner)
    step_three()
    conv(zhi + 1, 0)
    step_four()
    conv(zhi + 1, 1)
    collect(zhi + 1)
    for copy in above:
        copy.wait_recv()
    relay.wait_recv()
    base = near_plane * 1040

    def cap(i, carry):
        G[pl.ds(pl.multiple_of(base + (i + 1) * 40 + 8, 8), 24), :] = condition(HZ[i])
        return carry

    lax.fori_loop(0, 24, cap, 0)
    for s in (0, 1):
        G[pl.ds(pl.multiple_of(base + s * 1000 + 8, 8), 24), :] = jnp.where(
            x_ok[s], condition(HZX[s]), 0.0
        )
        G[pl.ds(base + 40 + 7 + s * 25, 24, stride=40), :] = jnp.where(
            y_ok[s], HZY[s].astype(F32), 0.0
        )
    for sx in (0, 1):
        for sy in (0, 1):
            there = HZC[sx * 2 + sy].astype(F32)
            cell = jnp.where(zhi == 0, there[0:1], there[11:12])
            G[pl.ds(base + sx * 1000 + 7 + sy * 25, 1), :] = jnp.where(
                x_ok[sx] & y_ok[sy], cell, 0.0
            )
    fill(near_plane)
    conv(2 - 2 * zhi, 0)
    conv(2 - 2 * zhi, 1)
    collect(2 - 2 * zhi)

    def regroup(upper, at):
        for part in range(4):
            block = slice(part * 16, part * 16 + 16)
            if upper:
                rows = WR[2:4, :, at, :, block, :].reshape(256, 256)
                lane = 64 + at * 16
            else:
                rows = WR[0:2, :, :, at, block, :].reshape(256, 256)
                lane = at * 16
            turned = jnp.dot(PM[...], rows, preferred_element_type=F32).astype(BF16)
            WP[block, pl.ds(pl.multiple_of(lane, 16), 16), :] = turned.reshape(16, 16, 256)

    for ring in (low_y[-1], low_y[1], low_y[0], low_y[2]):
        ring.finish()
    pass_low(2)
    for ring in (high_x[-1], high_x[1], high_x[0], high_x[2]):
        ring.finish()
    pass_high(2)
    for step in (0, -1, 1, 2):
        hand["low", step].wait_recv()
        regroup(0, (y + 4 + step) % 4)
        hand["high", step].wait_recv()
        regroup(1, (x + 4 + step) % 4)

    def project(i, total):
        lanes = pl.ds(pl.multiple_of(i * 1024, 1024), 1024)
        rows = WP[pl.ds(i * 8, 8)].reshape(1024, 256)
        return total + jnp.dot(HID[:, lanes], rows, preferred_element_type=F32)

    total = lax.fori_loop(0, 8, project, jnp.zeros((144, 256), F32))
    total = total + pbias[:, pl.ds(pl.multiple_of(zlo * 256, 256), 256)]
    total = total.astype(BF16).astype(F32)
    for h in range(2):
        CF[h] = total[:, h * 128 : h * 128 + 128]

    mine = FR.at[core]
    for cz in range(3):
        for cx in range(6):
            for h in range(2):
                mine[h, cz + 1, (cx + 1) * 8 + 1 : (cx + 1) * 8 + 7, :] = CF[
                    h, cz * 48 + cx * 6 : cz * 48 + cx * 6 + 6, :
                ]
    for cz in range(3):
        for h in range(2):
            YB[0, h, cz] = mine[h, cz + 1, pl.ds(1, 8, stride=8), :]
            YB[1, h, cz] = mine[h, cz + 1, pl.ds(6, 8, stride=8), :]
    top = 2 - 2 * zhi
    wide = {-1: 6, 1: 1}
    ZB[...] = mine[:, top + 1, 8:56].astype(BF16)
    for s in (0, 1):
        YZ[s] = YB[s, :, top].astype(BF16)
    XZ[0] = mine[:, top + 1, 8:16].astype(BF16)
    XZ[1] = mine[:, top + 1, 48:56].astype(BF16)
    around = []
    for sx in SIDES:
        for sy in SIDES:
            around.append(
                mail.post(YB.at[strip[sy]], CC.at[slot[sx] * 2 + slot[sy]], near(-sx, -sy, 0))
            )
    for s in SIDES:
        column = slice(wide[s] * 8, wide[s] * 8 + 8)
        around.append(mail.post(mine.at[:, 1:4, column], CX.at[slot[s]], near(-s, 0, 0)))
        around.append(mail.post(YB.at[strip[s]], CY.at[slot[s]], near(0, -s, 0)))
    beyond = []
    for sx in SIDES:
        for sy in SIDES:
            beyond.append(
                mail.post(YZ.at[strip[sy]], CZC.at[slot[sx] * 2 + slot[sy]], near(-sx, -sy, 1))
            )
    for s in SIDES:
        beyond.append(mail.post(XZ.at[strip[s]], CZX.at[slot[s]], near(-s, 0, 1)))
        beyond.append(mail.post(YZ.at[strip[s]], CZY.at[slot[s]], near(0, -s, 1)))
    beyond.append(mail.post(ZB, CZ, near(0, 0, 1)))
    for copy in around:
        copy.wait_send()
    for copy in around:
        copy.wait_recv()

    place8 = lax.broadcasted_iota(jnp.int32, (8, 128), 0)
    def frame(plane, in_x, in_y, in_corner):
        for s in (0, 1):
            plane[s * 56 : s * 56 + 8, :] = jnp.where(x_ok[s], in_x[s], 0.0)
        for s in (0, 1):
            low_row = jnp.broadcast_to(in_corner[s][6:7], (8, 128))
            high_row = jnp.broadcast_to(in_corner[2 + s][1:2], (8, 128))
            value = jnp.where(place8 == 0, jnp.where(x_ok[0], low_row, 0.0), in_y[s])
            value = jnp.where(place8 == 7, jnp.where(x_ok[1], high_row, 0.0), value)
            plane[pl.ds(s * 7, 8, stride=8), :] = jnp.where(y_ok[s], value, 0.0)

    for h in range(2):
        for cz in range(3):
            frame(
                mine.at[h, cz + 1],
                [CX[s, h, cz] for s in (0, 1)],
                [CY[s, h, cz] for s in (0, 1)],
                [CC[s, h, cz] for s in range(4)],
            )
    trade = mail.post(mine.at[:, 1:4], mine.at[:, 1:4], partner)

    def spread(w, put):
        for dy in range(3):
            turned = w if dy == 0 else pltpu.roll(w, 64 - dy, 0)
            for dx in range(3):
                put(dx * 3 + dy, turned[dx * 8 : dx * 8 + 48].astype(BF16))

    def lay(c, z, h):
        def put(i, rows):
            FB[i, c, z, :, h * 128 : h * 128 + 128] = rows

        spread(FR[c, h, z], put)

    def blank_ends(i, carry):
        for c in range(2):
            for z in (0, 4):
                FB[i, c, z] = jnp.zeros((48, 256), BF16)
        return carry

    lax.fori_loop(0, 9, blank_ends, 0)

    def stack_own(i, carry):
        for h in range(2):
            lay(core, i + 1, h)
        return carry

    lax.fori_loop(0, 3, stack_own, 0)
    trade.wait_recv()

    def stack_other(i, carry):
        for h in range(2):
            lay(1 - core, i + 1, h)
        return carry

    lax.fori_loop(0, 3, stack_other, 0)

    for copy in own_b:
        copy.wait()
    for copy in swap_b:
        copy.wait_recv()
    first_half = 1 - zlo // 2

    def columns(step):
        return pl.ds(pl.multiple_of(((first_half + step) % 2) * 256, 256), 256)

    def bottle(step):
        n = columns(step)
        T[step] = jnp.zeros((288, 256), F32)

        def taps(i, carry):
            total = T[step]
            for dz in range(3):
                rows = FB[i, :, dz : dz + 3].reshape(288, 256)
                total = total + jnp.dot(rows, BW[i * 3 + dz, :, n], preferred_element_type=F32)
            T[step] = total
            return carry

        lax.fori_loop(0, 9, taps, 0)

    def compact(step, cz):
        at = (first_half + step) % 2 * 2
        for c in range(2):
            for cx in range(6):
                row = pl.multiple_of(c * 144 + cz * 48 + cx * 8, 8)
                for j in range(2):
                    TS[at + j, cz, c, cx * 6 : cx * 6 + 6, :] = T[
                        step, pl.ds(row, 6), j * 128 : j * 128 + 128
                    ]

    across = [(first_half % 2) * 2 + (zlo + j) % 2 for j in range(2)]
    across.append((first_half + 1) % 2 * 2 + (zlo + 1) % 2)
    gather = []

    def ship(m, layers, static):
        for cz in static:
            for c in range(2):
                TB[m, cz, c] = TS[across[m], cz, c].astype(BF16)
        gather.append(
            mail.post(
                TB.at[m, layers], RB.at[m, layers], device_at(across[m], core, x, y, zhi)
            )
        )

    ready = pl.ds(zhi, 2)
    bottle(0)
    for cz in range(2):
        compact(0, zhi + cz)
    for m in (0, 1):
        ship(m, ready, (zhi, zhi + 1))
    bottle(1)
    for cz in range(2):
        compact(1, zhi + cz)
    ship(2, ready, (zhi, zhi + 1))

    for copy in beyond:
        copy.wait_recv()
    for h in range(2):
        ZF[core, h, 8:56, :] = CZ[h].astype(F32)
        frame(
            ZF.at[core, h],
            [CZX[s, h].astype(F32) for s in (0, 1)],
            [CZY[s, h].astype(F32) for s in (0, 1)],
            [CZC[s, h].astype(F32) for s in range(4)],
        )
    trade_z = mail.post(ZF.at[core], ZF.at[core], partner)
    trade_z.wait_recv()
    for c in range(2):
        for h in range(2):

            def put(i, rows, c=c, h=h):
                FZ[i, c * 48 : c * 48 + 48, h * 128 : h * 128 + 128] = rows

            spread(ZF[c, h], put)

    for step in range(2):
        n = columns(step)

        def cap_taps(i, total):
            return total + jnp.dot(FZ[i], BW[i * 3 + top, :, n], preferred_element_type=F32)

        extra = lax.fori_loop(0, 9, cap_taps, jnp.zeros((96, 256), F32))
        for c in range(2):
            at = pl.ds(pl.multiple_of(c * 144 + top * 48, 16), 48)
            T[step, at, :] = T[step, at, :] + extra[c * 48 : c * 48 + 48]
        compact(step, top)
        for m in ((0, 1), (2,))[step]:
            ship(m, top, (top,))
    for copy in gather:
        copy.wait_recv()
    lane = pl.ds(pl.multiple_of((zlo * 2 + core) * 128, 128), 128)
    for cz in range(3):
        result = []
        for c in range(2):
            value = TS[zlo, cz, c]
            for j in range(3):
                value = value + RB[j, cz, c].astype(F32)
            result.append(silu(value + bbias[:, lane]))
        OF[...] = result[0] + guide[0] * (result[1] - result[0])
        for cx in range(6):
            out[cz, cx, 0:6, :] = OF[cx * 6 : cx * 6 + 6, :].astype(BF16)
            out[cz, cx, 6:8, :] = jnp.zeros((2, 128), BF16)

    for copy in mail.all:
        copy.wait_send()


MESSAGES = 120


def shards(lat, scale, shift, fw, fbias, pw, pbias, bw, bbias, guide):
    anywhere = pl.BlockSpec(memory_space=pl.ANY)
    vmem = pl.BlockSpec(memory_space=pltpu.VMEM)
    scratch = [
        pltpu.VMEM((24, 12, 24, 128), BF16),
        pltpu.VMEM((14 * 1040, 128), F32),
        pltpu.VMEM((2, 3, 624, 14 * 128), BF16),
        pltpu.VMEM((27, 128, 128), BF16),
        pltpu.VMEM((9, 512, 256), BF16),
        pltpu.VMEM((4, 624, 128), F32),
        pltpu.VMEM((144, 8192), BF16),
        pltpu.VMEM((4, 2, 4, 4, 64, 256), BF16),
        pltpu.VMEM((64, 128, 256), BF16),
        pltpu.VMEM((256, 256), BF16),
        pltpu.VMEM((27, 256, 512), BF16),
        pltpu.VMEM((2, 144, 128), F32),
        pltpu.VMEM((2, 2, 5, 64, 128), F32),
        pltpu.VMEM((9, 2, 5, 48, 256), BF16),
        pltpu.VMEM((9, 96, 256), BF16),
        pltpu.VMEM((2, 2, 64, 128), F32),
        pltpu.VMEM((2, 288, 256), F32),
        pltpu.VMEM((4, 3, 2, 36, 128), F32),
        pltpu.VMEM((3, 3, 2, 36, 128), BF16),
        pltpu.VMEM((3, 3, 2, 36, 128), BF16),
        pltpu.VMEM((36, 128), F32),
        pltpu.VMEM((2, 2, 3, 8, 128), F32),
        pltpu.VMEM((2, 48, 128), BF16),
        pltpu.VMEM((2, 2, 8, 128), BF16),
        pltpu.VMEM((2, 2, 8, 128), BF16),
        pltpu.VMEM((2, 12, 24, 128), BF16),
        pltpu.VMEM((2, 12, 24, 128), BF16),
        pltpu.VMEM((4, 12, 128), BF16),
        pltpu.VMEM((2, 12, 24, 128), BF16),
        pltpu.VMEM((4, 12, 128), BF16),
        pltpu.VMEM((24, 24, 128), BF16),
        pltpu.VMEM((2, 24, 128), BF16),
        pltpu.VMEM((2, 24, 128), BF16),
        pltpu.VMEM((4, 12, 128), BF16),
        pltpu.VMEM((2, 2, 3, 8, 128), F32),
        pltpu.VMEM((2, 2, 3, 8, 128), F32),
        pltpu.VMEM((4, 2, 3, 8, 128), F32),
        pltpu.VMEM((2, 48, 128), BF16),
        pltpu.VMEM((2, 2, 8, 128), BF16),
        pltpu.VMEM((2, 2, 8, 128), BF16),
        pltpu.VMEM((4, 2, 8, 128), BF16),
        pltpu.SemaphoreType.DMA((16,)),
        pltpu.SemaphoreType.DMA((MESSAGES,)),
        pltpu.SemaphoreType.DMA((MESSAGES,)),
    ]
    rows = pl.pallas_call(
        kernel,
        out_shape=jax.ShapeDtypeStruct((3, 6, 8, 128), BF16),
        in_specs=[
            anywhere, vmem, vmem, anywhere, vmem, anywhere, vmem, anywhere, vmem,
            pl.BlockSpec(memory_space=pltpu.SMEM),
        ],
        out_specs=vmem,
        scratch_shapes=scratch,
        compiler_params=pltpu.CompilerParams(
            collective_id=0, has_side_effects=True, vmem_limit_bytes=67043328
        ),
        name="denoise",
    )(
        lat.transpose(0, 1, 3, 2, 4),
        scale.reshape(1, -1),
        shift.reshape(1, -1),
        fw.reshape(27, 128, 128),
        fbias.reshape(1, -1),
        pw,
        pbias.reshape(1, -1),
        bw,
        bbias.reshape(1, -1),
        guide,
    )
    return rows[:, :, :6].transpose(1, 2, 0, 3)[None]


def solution(mesh):
    placed = (
        P("region", None, None, None, None),
        P(),
        P(),
        P(),
        P(),
        P(("chan", "region"), None),
        P(),
        P(None, "chan", None),
        P(),
        P(),
    )
    return jax.shard_map(
        shards,
        mesh=mesh,
        in_specs=placed,
        out_specs=P("region", None, None, None, "chan"),
        check_vma=False,
    )
```

```python
import functools

import jax
import jax.numpy as jnp
from jax import lax
from jax.experimental import pallas as pl
from jax.experimental.pallas import tpu as pltpu
from jax.sharding import PartitionSpec as P

F32 = jnp.float32
BF16 = jnp.bfloat16
SIDES = (-1, 1)


def place_of():
    c = lax.axis_index("chan")
    r = lax.axis_index("region")
    return c // 2, c % 2, r // 8, r // 2 % 4, r % 2


def device_at(zlo, core, x, y, zhi):
    return (zlo * 2 + core, (x * 4 + y) * 2 + zhi)


class Parcel:
    def __init__(self, copy):
        self.copy, self.sent, self.received = copy, False, False

    def wait_send(self):
        if not self.sent:
            self.copy.wait_send()
        self.sent = True

    def wait_recv(self):
        if not self.received:
            self.copy.wait_recv()
        self.received = True


class Mail:
    def __init__(self, send, recv):
        self.send, self.recv = send, recv
        self.all = []

    def post(self, src, dst, target):
        copy = pltpu.make_async_remote_copy(
            src_ref=src,
            dst_ref=dst,
            send_sem=self.send.at[len(self.all)],
            recv_sem=self.recv.at[len(self.all)],
            device_id=target,
            device_id_type=pl.DeviceIdType.MESH,
        )
        copy.start()
        self.all.append(Parcel(copy))
        return self.all[-1]


def silu(v):
    return v / (1.0 + jnp.exp(-v))


def kernel(
    lat, scale, shift, fw, fbias, pw, pbias, bw, bbias, guide,
    out,
    L, G, A, FW, WZ, H, HID, WR, WP, PM, BW, CF, FR, FB, FZ, ZF, T, TS, TB, RB, OF, YB, ZB, YZ, XZ,
    HX, HY, HC, YS, CS, HZ, HZX, HZY, HZC,
    CX, CY, CC, CZ, CZX, CZY, CZC,
    lsem, ssem, rsem,
):
    zlo, core, x, y, zhi = place_of()
    mail = Mail(ssem, rsem)

    def near(sx, sy, sz):
        return device_at(zlo, core, (x + sx) % 4, (y + sy) % 4, (zhi + sz) % 2)

    def line(dz):
        z = (zhi * 4 + zlo + dz) % 8
        return device_at(z % 4, core, x, y, z // 4)

    partner = device_at(zlo, 1 - core, x, y, zhi)

    barrier = pltpu.get_barrier_semaphore()
    friends = [near(sx, sy, 0) for sx in (-1, 0, 1) for sy in (-1, 0, 1) if sx or sy]
    friends += [near(sx, sy, 1) for sx in (-1, 0, 1) for sy in (-1, 0, 1)]
    friends += [near(2, 0, 0), near(0, 2, 0)]
    friends += [line(d) for d in (1, 2, 3, 5, 6, 7)]
    friends += [partner]
    for friend in friends:
        pl.semaphore_signal(barrier, inc=1, device_id=friend, device_id_type=pl.DeviceIdType.MESH)

    loads = []

    def load(src, dst):
        copy = pltpu.make_async_copy(src, dst, lsem.at[len(loads)])
        copy.start()
        loads.append(copy)
        return copy

    load_lat = [load(lat.at[0, i * 6 : i * 6 + 6], L.at[i * 6 : i * 6 + 6]) for i in range(4)]
    load_fw = load(fw, FW)
    own_w = load(
        pw.at[:, pl.ds(pl.multiple_of(zlo * 256, 256), 256)],
        WR.at[zlo, core, x, y, pl.ds(pl.multiple_of(zhi * 32, 32), 32)],
    )
    pl.semaphore_wait(barrier, len(friends))

    rows_here = pl.ds(pl.multiple_of(zhi * 32, 32), 32)
    first = []
    for d in (4, 3, 5, 2, 6, 1, 7):
        z_there = (zhi * 4 + zlo + d) % 8 % 4
        first.append(
            mail.post(
                pw.at[:, pl.ds(pl.multiple_of(z_there * 256, 256), 256)],
                WR.at[zlo, core, x, y, rows_here],
                line(d),
            )
        )

    edge = {-1: 23, 1: 0}
    slot = {-1: 0, 1: 1}
    strip = {-1: 1, 1: 0}
    end = 11 - 11 * zhi
    fine = []
    for s in SIDES:
        fine.append(mail.post(lat.at[0, edge[s]], HX.at[slot[s]], near(-s, 0, 0)))

    gain = jnp.where(core == 1, scale[...], 1.0)
    offset = jnp.where(core == 1, shift[...], 0.0)

    def condition(values):
        return (values.astype(F32) * gain + offset).astype(BF16).astype(F32)

    def widen(i, carry):
        for z in range(12):
            at = pl.multiple_of(((z + 1) * 26 + i + 1) * 40 + 8, 8)
            G[pl.ds(at, 24), :] = condition(L[i, z])
        return carry

    for i in range(4):
        load_lat[i].wait()
        lax.fori_loop(i * 6, i * 6 + 6, widen, 0)

    def side(z, carry):
        at = ((z + 1) * 26 + 1) * 40 + 8
        YS[0, z] = G[pl.ds(at, 24, stride=40), :].astype(BF16)
        YS[1, z] = G[pl.ds(at + 23, 24, stride=40), :].astype(BF16)
        return carry

    lax.fori_loop(0, 12, side, 0)
    for sx in (0, 1):
        for sy in (0, 1):
            at = (26 + 1 + 23 * sx) * 40 + 8 + 23 * sy
            CS[sx * 2 + sy] = G[pl.ds(at, 12, stride=1040), :].astype(BF16)

    for s in SIDES:
        fine.append(mail.post(YS.at[strip[s]], HY.at[slot[s]], near(0, -s, 0)))
    for sx in SIDES:
        for sy in SIDES:
            fine.append(
                mail.post(
                    CS.at[strip[sx] * 2 + strip[sy]],
                    HC.at[slot[sx] * 2 + slot[sy]],
                    near(-sx, -sy, 0),
                )
            )
    load_fw.wait()
    from_ch = lax.broadcasted_iota(jnp.int32, (128, 128), 0)
    to_ch = lax.broadcasted_iota(jnp.int32, (128, 128), 1)
    group, member = to_ch >> 4, to_ch & 15
    low_ch = (member >> 2) * 16 + (member & 3) * 4 + group
    high_ch = 64 + (member >> 2) * 16 + (group - 4) * 4 + (member & 3)
    order = from_ch == jnp.where(group < 4, low_ch, high_ch)
    order16 = jnp.where(order, 1.0, 0.0).astype(BF16)

    def arrange(i, carry):
        WZ[i, 3 * 128 : 4 * 128, 0:128] = jnp.zeros((128, 128), BF16)
        WZ[i, 0:128, 128:256] = jnp.zeros((128, 128), BF16)
        for dz in range(3):
            tap = jnp.dot(FW[i * 3 + dz], order16, preferred_element_type=F32).astype(BF16)
            for o in range(2):
                at = (dz + o) * 128
                WZ[i, at : at + 128, o * 128 : o * 128 + 128] = tap
        return carry

    lax.fori_loop(0, 9, arrange, 0)
    bias = jnp.dot(
        jnp.broadcast_to(fbias[...], (8, 128)),
        jnp.where(order, 1.0, 0.0),
        preferred_element_type=F32,
        precision=lax.Precision.HIGHEST,
    )[0:1]
    bias = jnp.concatenate([bias, bias], axis=1)
    row = lax.broadcasted_iota(jnp.int32, (256, 256), 0)
    col = lax.broadcasted_iota(jnp.int32, (256, 256), 1)
    PM[...] = jnp.where(col == (row & 15) * 16 + (row >> 4), 1.0, 0.0).astype(BF16)
    H[:, 576:624, :] = jnp.zeros((4, 48, 128), F32)

    own_w.wait()
    for copy in first:
        copy.wait_recv()

    def low(j, x_at, y_at):
        return WR.at[j, core, x_at % 4, y_at % 4]

    def high(j, x_at, y_at):
        return low(j, x_at, y_at)

    both = {"low": slice(0, 2), "high": slice(2, 4)}
    base_of = {"low": 0, "high": 2}

    class Ring:
        def __init__(self, part, along_x, shift):
            self.part, self.along_x, self.shift = part, along_x, shift
            block = self.at(both[part], 0)
            self.up = mail.post(block, block, self.to(1))
            self.down = mail.post(block, block, self.to(-1))

        def at(self, j, step):
            if self.along_x:
                return low(j, x + 4 + step, y + 4 + self.shift)
            return low(j, x + 4 + self.shift, y + 4 + step)

        def to(self, step):
            return near(4 + step, 0, 0) if self.along_x else near(0, 4 + step, 0)

        def relay(self):
            self.up.wait_recv()
            piece = self.at(base_of[self.part], -1)
            self.up2 = mail.post(piece, piece, self.to(1))
            self.down.wait_recv()
            piece = self.at(base_of[self.part] + 1, 1)
            self.down2 = mail.post(piece, piece, self.to(-1))

        def finish(self):
            self.up2.wait_recv()
            self.down2.wait_recv()

    low_x = Ring("low", True, 0)
    high_y = Ring("high", False, 0)
    low_y = {0: Ring("low", False, 0)}
    high_x = {0: Ring("high", True, 0)}

    half = pl.ds(pl.multiple_of(core * 12, 12), 12)
    face = mail.post(lat.at[0, half, end], HZ.at[half], near(0, 0, 1))
    above = [mail.post(lat.at[0, edge[s], end], HZX.at[slot[s]], near(-s, 0, 1)) for s in SIDES]
    for s in SIDES:
        above.append(mail.post(YS.at[strip[s], end], HZY.at[slot[s]], near(0, -s, 1)))
    for sx in SIDES:
        for sy in SIDES:
            above.append(
                mail.post(
                    CS.at[strip[sx] * 2 + strip[sy]],
                    HZC.at[slot[sx] * 2 + slot[sy]],
                    near(-sx, -sy, 1),
                )
            )

    def step_one():
        low_x.relay()
        high_y.relay()
        for e in (-1, 1):
            low_y[e] = Ring("low", False, e)
            high_x[e] = Ring("high", True, e)
        low_y[0].relay()
        high_x[0].relay()

    def step_two():
        low_x.finish()
        high_y.finish()
        low_y[2] = Ring("low", False, 2)
        high_x[2] = Ring("high", True, 2)

    hand = {}

    def pass_low(step):
        column = WR.at[both["low"], core, :, (y + 4 + step) % 4]
        hand["low", step] = mail.post(column, column, partner)

    def pass_high(step):
        column = WR.at[both["high"], core, (x + 4 + step) % 4]
        hand["high", step] = mail.post(column, column, partner)

    def step_three():
        pass_low(0)
        pass_high(0)
        for e in (-1, 1):
            low_y[e].relay()
            high_x[e].relay()

    def step_four():
        low_y[2].relay()
        high_x[2].relay()
        for e in (-1, 1):
            pass_low(e)
            pass_high(e)

    for copy in fine:
        copy.wait_recv()
    x_ok = (x > 0, x < 3)
    y_ok = (y > 0, y < 3)

    def border(z, carry):
        base = (z + 1) * 1040
        for s in (0, 1):
            G[pl.ds(pl.multiple_of(base + s * 1000 + 8, 8), 24), :] = jnp.where(
                x_ok[s], condition(HX[s, z]), 0.0
            )
            G[pl.ds(base + 40 + 7 + s * 25, 24, stride=40), :] = jnp.where(
                y_ok[s], HY[s, z].astype(F32), 0.0
            )
        return carry

    lax.fori_loop(0, 12, border, 0)
    for sx in (0, 1):
        for sy in (0, 1):
            G[pl.ds(1040 + sx * 1000 + 7 + sy * 25, 12, stride=1040), :] = jnp.where(
                x_ok[sx] & y_ok[sy], HC[sx * 2 + sy].astype(F32), 0.0
            )

    def fill(z):
        lanes = pl.ds(pl.multiple_of(z * 128, 128), 128)
        for parity in range(2):
            for m in range(13 - parity):
                at = z * 1040 + (2 * m + parity) * 40 + 7
                for dy in range(3):
                    pair = jnp.concatenate(
                        [G[pl.ds(at + dy, 24), :], G[pl.ds(at + dy + 40, 24), :]], axis=0
                    )
                    A[parity, dy, m * 48 : m * 48 + 48, lanes] = pair.astype(BF16)

    def inner(z, carry):
        fill(z + 1)
        return carry

    lax.fori_loop(0, 12, inner, 0)

    def conv(cz, pair):
        start = pl.multiple_of((cz * 2 + pair) * 256, 256)
        total = None
        for dx in range(3):
            for dy in range(3):
                first_row = dx // 2 * 48
                term = jnp.dot(
                    A[dx % 2, dy, first_row : first_row + 576, pl.ds(start, 512)],
                    WZ[dx * 3 + dy],
                    preferred_element_type=F32,
                )
                total = term if total is None else total + term
        value = silu(total + bias)
        for i in range(24):
            at = (i % 4 * 6 + i // 4) * 24
            for o in range(2):
                H[pair * 2 + o, at : at + 24, :] = value[
                    i * 24 : i * 24 + 24, o * 128 : o * 128 + 128
                ]

    def collect(cz):
        for zo in range(4):
            for xo in range(4):
                for yo in range(4):
                    part = xo * 16 + yo * 4 + zo
                    HID[pl.ds(pl.multiple_of(cz * 48, 16), 48), part * 128 : part * 128 + 128] = H[
                        zo, pl.ds(xo * 144 + yo, 48, stride=4), :
                    ].astype(BF16)

    step_one()

    own_b = [
        load(
            bw.at[:, :, pl.ds(pl.multiple_of((2 * z + core) * 128, 128), 128)],
            BW.at[:, pl.ds(pl.multiple_of(core * 128, 128), 128), z * 128 : z * 128 + 128],
        )
        for z in range(4)
    ]
    swap_b = [
        mail.post(
            bw.at[:, :, pl.ds(pl.multiple_of((2 * z + 1 - core) * 128, 128), 128)],
            BW.at[:, pl.ds(pl.multiple_of(core * 128, 128), 128), z * 128 : z * 128 + 128],
            partner,
        )
        for z in range(4)
    ]

    near_plane = 13 - 13 * zhi

    def blank(i, carry):
        G[pl.ds(pl.multiple_of(zrow0 + i * 40, 8), 40), :] = jnp.zeros((40, 128), F32)
        return carry

    zrow0 = (13 - near_plane) * 1040
    lax.fori_loop(0, 26, blank, 0)
    fill(13 - near_plane)
    conv(zhi, 0)
    step_two()
    conv(zhi, 1)
    collect(zhi)
    face.wait_recv()
    relay = mail.post(HZ.at[half], HZ.at[half], partner)
    step_three()
    conv(zhi + 1, 0)
    step_four()
    conv(zhi + 1, 1)
    collect(zhi + 1)
    for copy in above:
        copy.wait_recv()
    relay.wait_recv()
    base = near_plane * 1040

    def cap(i, carry):
        G[pl.ds(pl.multiple_of(base + (i + 1) * 40 + 8, 8), 24), :] = condition(HZ[i])
        return carry

    lax.fori_loop(0, 24, cap, 0)
    for s in (0, 1):
        G[pl.ds(pl.multiple_of(base + s * 1000 + 8, 8), 24), :] = jnp.where(
            x_ok[s], condition(HZX[s]), 0.0
        )
        G[pl.ds(base + 40 + 7 + s * 25, 24, stride=40), :] = jnp.where(
            y_ok[s], HZY[s].astype(F32), 0.0
        )
    for sx in (0, 1):
        for sy in (0, 1):
            there = HZC[sx * 2 + sy].astype(F32)
            cell = jnp.where(zhi == 0, there[0:1], there[11:12])
            G[pl.ds(base + sx * 1000 + 7 + sy * 25, 1), :] = jnp.where(
                x_ok[sx] & y_ok[sy], cell, 0.0
            )
    fill(near_plane)
    conv(2 - 2 * zhi, 0)
    conv(2 - 2 * zhi, 1)
    collect(2 - 2 * zhi)

    def regroup(upper, at):
        for part in range(4):
            block = slice(part * 16, part * 16 + 16)
            if upper:
                rows = WR[2:4, :, at, :, block, :].reshape(256, 256)
                lane = 64 + at * 16
            else:
                rows = WR[0:2, :, :, at, block, :].reshape(256, 256)
                lane = at * 16
            turned = jnp.dot(PM[...], rows, preferred_element_type=F32).astype(BF16)
            WP[block, pl.ds(pl.multiple_of(lane, 16), 16), :] = turned.reshape(16, 16, 256)

    def regroup_from(step):
        hand["low", step].wait_recv()
        regroup(0, (y + 4 + step) % 4)
        hand["high", step].wait_recv()
        regroup(1, (x + 4 + step) % 4)

    for step in (0, -1, 1):
        regroup_from(step)
    for ring in (low_y[-1], low_y[1], low_y[0], low_y[2]):
        ring.finish()
    pass_low(2)
    for ring in (high_x[-1], high_x[1], high_x[0], high_x[2]):
        ring.finish()
    pass_high(2)
    regroup_from(2)

    def project(i, total):
        lanes = pl.ds(pl.multiple_of(i * 1024, 1024), 1024)
        rows = WP[pl.ds(i * 8, 8)].reshape(1024, 256)
        return total + jnp.dot(HID[:, lanes], rows, preferred_element_type=F32)

    total = lax.fori_loop(0, 8, project, jnp.zeros((144, 256), F32))
    total = total + pbias[:, pl.ds(pl.multiple_of(zlo * 256, 256), 256)]
    total = total.astype(BF16).astype(F32)
    for h in range(2):
        CF[h] = total[:, h * 128 : h * 128 + 128]

    mine = FR.at[core]
    for cz in range(3):
        for cx in range(6):
            for h in range(2):
                mine[h, cz + 1, (cx + 1) * 8 + 1 : (cx + 1) * 8 + 7, :] = CF[
                    h, cz * 48 + cx * 6 : cz * 48 + cx * 6 + 6, :
                ]
    for cz in range(3):
        for h in range(2):
            YB[0, h, cz] = mine[h, cz + 1, pl.ds(1, 8, stride=8), :]
            YB[1, h, cz] = mine[h, cz + 1, pl.ds(6, 8, stride=8), :]
    top = 2 - 2 * zhi
    wide = {-1: 6, 1: 1}
    ZB[...] = mine[:, top + 1, 8:56].astype(BF16)
    for s in (0, 1):
        YZ[s] = YB[s, :, top].astype(BF16)
    XZ[0] = mine[:, top + 1, 8:16].astype(BF16)
    XZ[1] = mine[:, top + 1, 48:56].astype(BF16)
    around = []
    for sx in SIDES:
        for sy in SIDES:
            around.append(
                mail.post(YB.at[strip[sy]], CC.at[slot[sx] * 2 + slot[sy]], near(-sx, -sy, 0))
            )
    for s in SIDES:
        column = slice(wide[s] * 8, wide[s] * 8 + 8)
        around.append(mail.post(mine.at[:, 1:4, column], CX.at[slot[s]], near(-s, 0, 0)))
        around.append(mail.post(YB.at[strip[s]], CY.at[slot[s]], near(0, -s, 0)))
    beyond = []
    for sx in SIDES:
        for sy in SIDES:
            beyond.append(
                mail.post(YZ.at[strip[sy]], CZC.at[slot[sx] * 2 + slot[sy]], near(-sx, -sy, 1))
            )
    for s in SIDES:
        beyond.append(mail.post(XZ.at[strip[s]], CZX.at[slot[s]], near(-s, 0, 1)))
        beyond.append(mail.post(YZ.at[strip[s]], CZY.at[slot[s]], near(0, -s, 1)))
    beyond.append(mail.post(ZB, CZ, near(0, 0, 1)))
    for copy in around:
        copy.wait_send()
    for copy in around:
        copy.wait_recv()

    place8 = lax.broadcasted_iota(jnp.int32, (8, 128), 0)
    def frame(plane, in_x, in_y, in_corner):
        for s in (0, 1):
            plane[s * 56 : s * 56 + 8, :] = jnp.where(x_ok[s], in_x[s], 0.0)
        for s in (0, 1):
            low_row = jnp.broadcast_to(in_corner[s][6:7], (8, 128))
            high_row = jnp.broadcast_to(in_corner[2 + s][1:2], (8, 128))
            value = jnp.where(place8 == 0, jnp.where(x_ok[0], low_row, 0.0), in_y[s])
            value = jnp.where(place8 == 7, jnp.where(x_ok[1], high_row, 0.0), value)
            plane[pl.ds(s * 7, 8, stride=8), :] = jnp.where(y_ok[s], value, 0.0)

    for h in range(2):
        for cz in range(3):
            frame(
                mine.at[h, cz + 1],
                [CX[s, h, cz] for s in (0, 1)],
                [CY[s, h, cz] for s in (0, 1)],
                [CC[s, h, cz] for s in range(4)],
            )
    trade = mail.post(mine.at[:, 1:4], mine.at[:, 1:4], partner)

    def spread(w, put):
        for dy in range(3):
            turned = w if dy == 0 else pltpu.roll(w, 64 - dy, 0)
            for dx in range(3):
                put(dx * 3 + dy, turned[dx * 8 : dx * 8 + 48].astype(BF16))

    def lay(c, z, h):
        def put(i, rows):
            FB[i, c, z, :, h * 128 : h * 128 + 128] = rows

        spread(FR[c, h, z], put)

    def blank_ends(i, carry):
        for c in range(2):
            for z in (0, 4):
                FB[i, c, z] = jnp.zeros((48, 256), BF16)
        return carry

    lax.fori_loop(0, 9, blank_ends, 0)

    def stack_own(i, carry):
        for h in range(2):
            lay(core, i + 1, h)
        return carry

    lax.fori_loop(0, 3, stack_own, 0)
    trade.wait_recv()

    def stack_other(i, carry):
        for h in range(2):
            lay(1 - core, i + 1, h)
        return carry

    lax.fori_loop(0, 3, stack_other, 0)

    for copy in own_b:
        copy.wait()
    for copy in swap_b:
        copy.wait_recv()
    first_half = 1 - zlo // 2

    def columns(step):
        return pl.ds(pl.multiple_of(((first_half + step) % 2) * 256, 256), 256)

    def bottle(step):
        n = columns(step)
        T[step] = jnp.zeros((288, 256), F32)

        def taps(i, carry):
            total = T[step]
            for dz in range(3):
                rows = FB[i, :, dz : dz + 3].reshape(288, 256)
                total = total + jnp.dot(rows, BW[i * 3 + dz, :, n], preferred_element_type=F32)
            T[step] = total
            return carry

        lax.fori_loop(0, 9, taps, 0)

    def compact(step, cz):
        at = (first_half + step) % 2 * 2
        for c in range(2):
            for cx in range(6):
                row = pl.multiple_of(c * 144 + cz * 48 + cx * 8, 8)
                for j in range(2):
                    TS[at + j, cz, c, cx * 6 : cx * 6 + 6, :] = T[
                        step, pl.ds(row, 6), j * 128 : j * 128 + 128
                    ]

    across = [(first_half % 2) * 2 + (zlo + j) % 2 for j in range(2)]
    across.append((first_half + 1) % 2 * 2 + (zlo + 1) % 2)
    gather = []

    def ship(m, layers, static):
        for cz in static:
            for c in range(2):
                TB[m, cz, c] = TS[across[m], cz, c].astype(BF16)
        gather.append(
            mail.post(
                TB.at[m, layers], RB.at[m, layers], device_at(across[m], core, x, y, zhi)
            )
        )

    ready = pl.ds(zhi, 2)
    bottle(0)
    for cz in range(2):
        compact(0, zhi + cz)
    for m in (0, 1):
        ship(m, ready, (zhi, zhi + 1))
    bottle(1)
    for cz in range(2):
        compact(1, zhi + cz)
    ship(2, ready, (zhi, zhi + 1))

    for copy in beyond:
        copy.wait_recv()
    for h in range(2):
        ZF[core, h, 8:56, :] = CZ[h].astype(F32)
        frame(
            ZF.at[core, h],
            [CZX[s, h].astype(F32) for s in (0, 1)],
            [CZY[s, h].astype(F32) for s in (0, 1)],
            [CZC[s, h].astype(F32) for s in range(4)],
        )
    trade_z = mail.post(ZF.at[core], ZF.at[core], partner)
    trade_z.wait_recv()
    for c in range(2):
        for h in range(2):

            def put(i, rows, c=c, h=h):
                FZ[i, c * 48 : c * 48 + 48, h * 128 : h * 128 + 128] = rows

            spread(ZF[c, h], put)

    for step in range(2):
        n = columns(step)

        def cap_taps(i, total):
            return total + jnp.dot(FZ[i], BW[i * 3 + top, :, n], preferred_element_type=F32)

        extra = lax.fori_loop(0, 9, cap_taps, jnp.zeros((96, 256), F32))
        for c in range(2):
            at = pl.ds(pl.multiple_of(c * 144 + top * 48, 16), 48)
            T[step, at, :] = T[step, at, :] + extra[c * 48 : c * 48 + 48]
        compact(step, top)
        for m in ((0, 1), (2,))[step]:
            ship(m, top, (top,))
    for copy in gather:
        copy.wait_recv()
    lane = pl.ds(pl.multiple_of((zlo * 2 + core) * 128, 128), 128)
    for cz in range(3):
        result = []
        for c in range(2):
            value = TS[zlo, cz, c]
            for j in range(3):
                value = value + RB[j, cz, c].astype(F32)
            result.append(silu(value + bbias[:, lane]))
        OF[...] = result[0] + guide[0] * (result[1] - result[0])
        for cx in range(6):
            out[cz, cx, 0:6, :] = OF[cx * 6 : cx * 6 + 6, :].astype(BF16)
            out[cz, cx, 6:8, :] = jnp.zeros((2, 128), BF16)

    for copy in mail.all:
        copy.wait_send()


MESSAGES = 120


def shards(lat, scale, shift, fw, fbias, pw, pbias, bw, bbias, guide):
    anywhere = pl.BlockSpec(memory_space=pl.ANY)
    vmem = pl.BlockSpec(memory_space=pltpu.VMEM)
    scratch = [
        pltpu.VMEM((24, 12, 24, 128), BF16),
        pltpu.VMEM((14 * 1040, 128), F32),
        pltpu.VMEM((2, 3, 624, 14 * 128), BF16),
        pltpu.VMEM((27, 128, 128), BF16),
        pltpu.VMEM((9, 512, 256), BF16),
        pltpu.VMEM((4, 624, 128), F32),
        pltpu.VMEM((144, 8192), BF16),
        pltpu.VMEM((4, 2, 4, 4, 64, 256), BF16),
        pltpu.VMEM((64, 128, 256), BF16),
        pltpu.VMEM((256, 256), BF16),
        pltpu.VMEM((27, 256, 512), BF16),
        pltpu.VMEM((2, 144, 128), F32),
        pltpu.VMEM((2, 2, 5, 64, 128), F32),
        pltpu.VMEM((9, 2, 5, 48, 256), BF16),
        pltpu.VMEM((9, 96, 256), BF16),
        pltpu.VMEM((2, 2, 64, 128), F32),
        pltpu.VMEM((2, 288, 256), F32),
        pltpu.VMEM((4, 3, 2, 36, 128), F32),
        pltpu.VMEM((3, 3, 2, 36, 128), BF16),
        pltpu.VMEM((3, 3, 2, 36, 128), BF16),
        pltpu.VMEM((36, 128), F32),
        pltpu.VMEM((2, 2, 3, 8, 128), F32),
        pltpu.VMEM((2, 48, 128), BF16),
        pltpu.VMEM((2, 2, 8, 128), BF16),
        pltpu.VMEM((2, 2, 8, 128), BF16),
        pltpu.VMEM((2, 12, 24, 128), BF16),
        pltpu.VMEM((2, 12, 24, 128), BF16),
        pltpu.VMEM((4, 12, 128), BF16),
        pltpu.VMEM((2, 12, 24, 128), BF16),
        pltpu.VMEM((4, 12, 128), BF16),
        pltpu.VMEM((24, 24, 128), BF16),
        pltpu.VMEM((2, 24, 128), BF16),
        pltpu.VMEM((2, 24, 128), BF16),
        pltpu.VMEM((4, 12, 128), BF16),
        pltpu.VMEM((2, 2, 3, 8, 128), F32),
        pltpu.VMEM((2, 2, 3, 8, 128), F32),
        pltpu.VMEM((4, 2, 3, 8, 128), F32),
        pltpu.VMEM((2, 48, 128), BF16),
        pltpu.VMEM((2, 2, 8, 128), BF16),
        pltpu.VMEM((2, 2, 8, 128), BF16),
        pltpu.VMEM((4, 2, 8, 128), BF16),
        pltpu.SemaphoreType.DMA((16,)),
        pltpu.SemaphoreType.DMA((MESSAGES,)),
        pltpu.SemaphoreType.DMA((MESSAGES,)),
    ]
    rows = pl.pallas_call(
        kernel,
        out_shape=jax.ShapeDtypeStruct((3, 6, 8, 128), BF16),
        in_specs=[
            anywhere, vmem, vmem, anywhere, vmem, anywhere, vmem, anywhere, vmem,
            pl.BlockSpec(memory_space=pltpu.SMEM),
        ],
        out_specs=vmem,
        scratch_shapes=scratch,
        compiler_params=pltpu.CompilerParams(
            collective_id=0, has_side_effects=True, vmem_limit_bytes=67043328
        ),
        name="denoise",
    )(
        lat.transpose(0, 1, 3, 2, 4),
        scale.reshape(1, -1),
        shift.reshape(1, -1),
        fw.reshape(27, 128, 128),
        fbias.reshape(1, -1),
        pw,
        pbias.reshape(1, -1),
        bw,
        bbias.reshape(1, -1),
        guide,
    )
    return rows[:, :, :6].transpose(1, 2, 0, 3)[None]


def solution(mesh):
    placed = (
        P("region", None, None, None, None),
        P(),
        P(),
        P(),
        P(),
        P(("chan", "region"), None),
        P(),
        P(None, "chan", None),
        P(),
        P(),
    )
    return jax.shard_map(
        shards,
        mesh=mesh,
        in_specs=placed,
        out_specs=P("region", None, None, None, "chan"),
        check_vma=False,
    )
```
